128 devices in a mesh: wide: 32 (over x, z, core), narrow: 4 (over y).
Axes of the slice: x: 4, y: 4, z: 4, core: 2. Of those that a mesh axis runs over, the one named last changes fastest.
Arguments:
- amplitudes: float32 [16384, 1024], P('wide', 'narrow'), may hold values from -6 to 6
- ladder_blocks: float32 [128, 16, 128, 128], P('wide'), may hold values from -0.125 to 0.125
- ladder_index: int32 [128, 16], P('wide'), may hold values from 0 to 127, all different within a row
- cycle_blocks: float32 [32, 16, 128, 128], P(None, 'narrow'), may hold values from -0.125 to 0.125
- cycle_index: int32 [32, 16], P(None, 'narrow'), may hold values from 0 to 31, all different within a row
- eps_virt: float32 [128], replicated, may hold values from 0.3 to 1.5
- eps_occ: float32 [32], replicated, may hold values from -0.7 to -0.2
Outputs:
- new_amplitudes: float32 [16384, 1024], P('wide', 'narrow')
The draws below stay inside these ranges and needn't reach their ends.
Inputs may be any that keep to these rules, and one draw needn't show every extreme that they name: `ladder_index`: each row lists 16 different virtual indices, and every virtual index is listed by some row. `cycle_index`: each row lists 16 different occupied indices, and every occupied index is listed by some row.
All inputs are finite; a program needn't handle non-finite values.
Results may differ from the reference program's by a relative error of at most 0.000052.
Values sent between devices are 32-bit elements; how exact they have to be, the bound alone decides.
A program may use at most 128 MiB of HBM per device.

```python
import jax
import jax.numpy as jnp
from jax import lax

V = 128
O = 32
LLIST = 16
RLIST = 16
PAIRS_V = 16384
PAIRS_O = 1024


def shard_levels(stream_key, extent, cuts, low, largest):
    level = 1.0
    for position, parts in cuts:
        heights = jax.random.uniform(jax.random.fold_in(jax.random.fold_in(stream_key, 6), position), (parts,), jnp.float32, low / len(cuts), largest / len(cuts))
        level = level * jnp.repeat(jnp.exp(heights), extent[position] // parts).reshape((-1,) + (1,) * (len(extent) - 1 - position))
    return level


def different_ones(own_key, rows, count, top, lift):
    sequence = jax.random.permutation(jax.random.fold_in(own_key, 1), count)
    boost = sequence
    for power in range(3):
        boost = boost * boost // count
    boost = boost * lift // count
    lots = jax.random.randint(jax.random.fold_in(own_key, 2), (rows, count), 0, 4096) + boost
    holders = jax.random.permutation(jax.random.fold_in(own_key, 3), rows)[jnp.arange(count) % rows]
    lots = jnp.where(jnp.arange(rows)[:, None] == holders[None, :], 1 << 14, lots)
    priority = lots * count + jnp.arange(count)
    return lax.top_k(priority.astype(jnp.int32), top)[1].astype(jnp.int32)


def gaussian(own_key, shape, scale, bound, shards=(), kind=jnp.bfloat16):
    entries = jax.random.normal(own_key, shape, jnp.float32) * scale
    if len(shards) > 0:
        entries = shard_levels(own_key, shape, shards, -0.22, 0.18) * entries
    return jnp.clip(entries, min=-bound, max=bound).astype(kind)


def setup_inputs(seed: int = 0) -> dict:
    arg_keys = jax.random.split(jax.random.key(seed), 8)
    amplitudes = gaussian(arg_keys[0], (PAIRS_V, PAIRS_O), 1.0, 6.0, ((0, 32), (1, 4)), jnp.float32)
    ladder_blocks = gaussian(arg_keys[1], (V, LLIST, V, V), (LLIST * V) ** -0.5, 0.125, ((0, 32),), jnp.float32)
    ladder_index = different_ones(arg_keys[2], V, V, LLIST, 0)
    cycle_blocks = gaussian(arg_keys[3], (O, RLIST, V, V), (RLIST * V) ** -0.5, 0.125, ((1, 4),), jnp.float32)
    cycle_index = different_ones(arg_keys[4], O, O, RLIST, 4096)
    eps_virt = jnp.clip(jax.random.uniform(arg_keys[5], (V,), jnp.float32, 0.3, 1.5), 0.3, 1.5)
    eps_occ = jnp.clip(jax.random.uniform(arg_keys[6], (O,), jnp.float32, -0.7, -0.2), -0.7, -0.2)
    return {"amplitudes": amplitudes, "ladder_blocks": ladder_blocks, "ladder_index": ladder_index, "cycle_blocks": cycle_blocks, "cycle_index": cycle_index, "eps_virt": eps_virt, "eps_occ": eps_occ}


def reference(amplitudes, ladder_blocks, ladder_index, cycle_blocks, cycle_index, eps_virt, eps_occ):
    by_virtual = amplitudes.reshape(V, V, O * O)

    def ladder_row(args):
        blocks, listed = args
        taken = by_virtual[listed]
        return jnp.einsum("kbd,kdn->bn", blocks, taken, precision=lax.Precision.HIGHEST)

    ladder = lax.map(ladder_row, (ladder_blocks, ladder_index)).reshape(V * V, O * O)
    amp_four = amplitudes.reshape(V, V, O, O)
    by_occupied = amp_four.transpose(2, 0, 1, 3).reshape(O, V, V * O)

    def cycle_row(args):
        blocks, listed = args
        taken = by_occupied[listed]
        return jnp.einsum("sac,scn->an", blocks, taken, precision=lax.Precision.HIGHEST)

    cycle_ph = lax.map(cycle_row, (cycle_blocks, cycle_index))
    cycle = cycle_ph.reshape(O, V, V, O).transpose(1, 2, 0, 3).reshape(V * V, O * O)
    denominator = (eps_virt[:, None, None, None] + eps_virt[None, :, None, None]
                   - eps_occ[None, None, :, None] - eps_occ[None, None, None, :])
    return (ladder + cycle) / denominator.reshape(V * V, O * O)
```

```python
import functools

import jax
import jax.numpy as jnp
from jax import lax
from jax.experimental import pallas as pl
from jax.experimental.pallas import tpu as pltpu
from jax.sharding import PartitionSpec as P

MESH = pl.DeviceIdType.MESH
F32 = jnp.float32
BF16 = jnp.bfloat16
SIDE = 4
SLOTS = 15
AHEAD = 4

X_PLUS = (
    (0, 0, 0), (0, 0, 1), (0, 0, 2), (0, 0, 3), (-1, 0, 0),
    (0, -1, 2), (0, -1, 3), (0, 1, 2), (0, 1, 3), (0, 2, 2), (0, 2, 3),
    (-1, 0, 2), (-1, -1, 2), (-1, 1, 2), (-1, 2, 2),
)
X_MINUS = tuple((-dx, -dz, r ^ 1) for dx, dz, r in X_PLUS)
Z_PLUS = tuple((dz, dx, r ^ 2) for dx, dz, r in X_PLUS)
Z_MINUS = tuple((dz, dx, r ^ 2) for dx, dz, r in X_MINUS)
STREAMS = (X_PLUS, X_MINUS, Z_PLUS, Z_MINUS)
STEPS = ((1, 0), (-1, 0), (0, 1), (0, -1))


def digits(values):
    return sum((value % SIDE) << (2 * position) for position, value in enumerate(values))


SEND = tuple(
    tuple(digits([item[part] for item in stream]) for part in range(3)) for stream in STREAMS
)
ARRIVE = tuple(
    tuple(
        digits([item[part] - (step[part] if part < 2 else 0) for item in stream])
        for part in range(3)
    )
    for stream, step in zip(STREAMS, STEPS)
)


def digit(packed, position):
    return lax.rem(lax.shift_right_logical(packed, 2 * position), SIDE)


def split(value):
    high = value.astype(BF16)
    return high, (value - high.astype(F32)).astype(BF16)


def dot(left, right):
    return jnp.dot(left, right, preferred_element_type=F32)


def kernel(
    inv_ref, cidx_ref, ev_ref, t_ref, lad_ref, cyc_ref, ecol_ref, erow_ref, out_ref,
    gath, lhi, llo, lstage, cyc, turn, snd, got, thi, tlo, part, rbuf, zsend, zgot, acc,
    s_own, r_gath, s_gath, s_sib, s_lad, s_cyc, s_a2a, r_a2a, s_y, r_y, s_rs, r_rs, s_back, r_back,
):
    w = lax.axis_index("wide")
    n = lax.axis_index("narrow")
    core = lax.rem(w, 2)
    chip = w // 2
    x = chip // SIDE
    z = lax.rem(chip, SIDE)
    sib = w + 1 - 2 * core
    up = lax.rem(n + 1, SIDE)
    down = lax.rem(n + 3, SIDE)
    far = lax.rem(n + 2, SIDE)
    wide = 32

    def wide_of(dx, dz):
        return (lax.rem(x + dx, SIDE) * SIDE + lax.rem(z + dz, SIDE)) * 2 + core

    neighbours = [wide_of(step[0] % SIDE, step[1] % SIDE) for step in STEPS]

    def chunk(packed, position):
        return wide_of(digit(packed[0], position), digit(packed[1], position)) * 4 + digit(
            packed[2], position
        )

    def plane_copy(c, target, send_sem):
        return pltpu.make_async_remote_copy(
            src_ref=gath.at[c], dst_ref=gath.at[c], send_sem=send_sem, recv_sem=r_gath.at[c],
            device_id=(target, n), device_id_type=MESH,
        )

    own = pltpu.make_async_copy(t_ref, gath.at[pl.ds(w * 4, 4)], s_own)
    own.start()

    def lad_load(a):
        return pltpu.make_async_copy(lad_ref.at[a], lstage.at[a % 2], s_lad.at[a % 2])

    lad_load(0).start()
    lad_load(1).start()
    cyc_load = pltpu.make_async_copy(cyc_ref, cyc, s_cyc)
    cyc_load.start()

    barrier = pltpu.get_barrier_semaphore()

    @pl.loop(1, wide)
    def _(k):
        pl.semaphore_signal(
            barrier, inc=1, device_id=(lax.rem(w + k, wide), n), device_id_type=MESH
        )

    for other in (up, down):
        pl.semaphore_signal(barrier, inc=1, device_id=(w, other), device_id_type=MESH)

    own.wait()
    for c in range(4):
        turn[c * 256:(c + 1) * 256, :] = gath[w * 4 + c].T

    @pl.loop(0, wide)
    def _(j):
        for c in range(4):
            row = pl.multiple_of(j * 32 + c * 8, 8)
            snd[pl.ds(row, 8), :] = turn[pl.ds(c * 256 + j, 8, stride=32), :]

    mine = pl.multiple_of(w * 32, 32)
    got[n, pl.ds(mine, 32), :] = snd[pl.ds(mine, 32), :]

    pl.semaphore_wait(barrier, wide + 1)

    def a2a(k):
        target = lax.rem(w + k, wide)
        return pltpu.make_async_remote_copy(
            src_ref=snd.at[pl.ds(pl.multiple_of(target * 32, 32), 32)],
            dst_ref=got.at[n, pl.ds(mine, 32)],
            send_sem=s_a2a.at[k], recv_sem=r_a2a.at[w],
            device_id=(target, n), device_id_type=MESH,
        )

    def a2a_in(k):
        source = lax.rem(w + k, wide)
        place = got.at[n, pl.ds(pl.multiple_of(source * 32, 32), 32)]
        return pltpu.make_async_copy(place, place, r_a2a.at[source])

    @pl.loop(1, wide)
    def _(k):
        a2a(k).start()

    @pl.loop(0, AHEAD)
    def _(s):
        for d in range(4):
            plane_copy(chunk(SEND[d], s), neighbours[d], s_gath.at[d, s]).start()

    @pl.loop(0, 4)
    def _(r):
        plane_copy(w * 4 + r, sib, s_sib.at[60 + r]).start()

    for a in range(4):
        lad_load(a).wait()

        @pl.loop(0, 16)
        def _(s):
            high, low = split(lstage[a % 2, s])
            lhi[a * 17 + s] = high
            llo[a * 17 + s] = low

        lhi[a * 17 + 16] = jnp.zeros((128, 128), BF16)
        llo[a * 17 + 16] = jnp.zeros((128, 128), BF16)
        if a < 2:
            lad_load(a + 2).start()
    acc[...] = jnp.zeros_like(acc)

    half = 512

    def y_copy(direction, item):
        where, piece = {
            (0, 0): (n, 0), (0, 1): (n, 1), (0, 2): (down, 0),
            (1, 0): (n, 1), (1, 1): (n, 0), (1, 2): (up, 1),
        }[(direction, item)]
        place = got.at[where, pl.ds(piece * half, half)]
        return pltpu.make_async_remote_copy(
            src_ref=place, dst_ref=place, send_sem=s_y.at[direction, item],
            recv_sem=r_y.at[direction, item],
            device_id=(w, up if direction == 0 else down), device_id_type=MESH,
        )

    def y_in(direction, item):
        place = got.at[0, pl.ds(0, half)]
        return pltpu.make_async_copy(place, place, r_y.at[direction, item])

    @pl.loop(1, wide)
    def _(k):
        a2a_in(k).wait()

    for item in range(2):
        for direction in range(2):
            y_copy(direction, item).start()

    def spread(slice_of):
        for k in range(8):
            high, low = split(got[slice_of, pl.ds(k, 128, stride=8), :])
            thi[slice_of * 8 + k] = high
            tlo[slice_of * 8 + k] = low

    def cycle_terms(slice_of, piece):
        @pl.loop(0, 4)
        def _(ii):
            i = slice_of * 8 + piece * 4 + ii
            blocks = [split(cyc[i, s]) for s in range(4)]
            left_high = jnp.concatenate([b[0] for b in blocks], axis=1)
            left_low = jnp.concatenate([b[1] for b in blocks], axis=1)
            listed = [cidx_ref[i, s] for s in range(4)]
            right_high = jnp.concatenate([thi[k] for k in listed], axis=0)
            right_low = jnp.concatenate([tlo[k] for k in listed], axis=0)
            part[slice_of, piece, ii] = (
                dot(left_high, right_high) + dot(left_low, right_high) + dot(left_high, right_low)
            )

    def rs_copy(direction, item):
        source = {
            (0, 0): (far, 0), (0, 1): (up, 1), (0, 2): (up, 0),
            (1, 0): (far, 1), (1, 1): (down, 0), (1, 2): (down, 1),
        }[(direction, item)]
        return pltpu.make_async_remote_copy(
            src_ref=part.at[source[0], source[1]], dst_ref=rbuf.at[direction, item],
            send_sem=s_rs.at[direction, item], recv_sem=r_rs.at[direction, item],
            device_id=(w, up if direction == 0 else down), device_id_type=MESH,
        )

    def pair(c):
        other = c + 4 - 8 * core
        high_0, low_0 = split(gath[c])
        high_1, low_1 = split(gath[other])
        high = jnp.concatenate([high_0, high_1], axis=0)
        low = jnp.concatenate([low_0, low_1], axis=0)

        def taken(table):
            return jnp.concatenate(
                [
                    jnp.concatenate(
                        [table[a * 17 + inv_ref[a, c]], table[a * 17 + inv_ref[a, other]]], axis=1
                    )
                    for a in range(4)
                ],
                axis=0,
            )

        left_high, left_low = taken(lhi), taken(llo)
        acc[...] += dot(left_high, high) + dot(left_low, high) + dot(left_high, low)

    def sibling_in(c):
        other = c + 4 - 8 * core
        pltpu.make_async_copy(gath.at[other], gath.at[other], r_gath.at[other]).wait()

    @pl.loop(0, SLOTS + 1)
    def _(q):
        @pl.when(q < SLOTS)
        def _():
            for d in range(4):
                c = chunk(ARRIVE[d], q)
                pltpu.make_async_copy(gath.at[c], gath.at[c], r_gath.at[c]).wait()
                plane_copy(c, sib, s_sib.at[4 * q + d]).start()

        @pl.when(q < SLOTS - AHEAD)
        def _():
            for d in range(4):
                plane_copy(
                    chunk(SEND[d], q + AHEAD), neighbours[d], s_gath.at[d, q + AHEAD]
                ).start()

        @pl.when(q == 2)
        def _():
            for direction in range(2):
                y_in(direction, 0).wait()
            for direction in range(2):
                y_copy(direction, 2).start()
            spread(n)

        @pl.when(q == 4)
        def _():
            for direction in range(2):
                y_in(direction, 1).wait()
            spread(up)
            spread(down)

        @pl.when(q == 6)
        def _():
            cyc_load.wait()
            for direction in range(2):
                y_in(direction, 2).wait()
            spread(far)
            for direction in range(2):
                cycle_terms(far, direction)
                rs_copy(direction, 0).start()

        @pl.when(q == 7)
        def _():
            cycle_terms(up, 1)
            rs_copy(0, 1).start()
            cycle_terms(down, 0)
            rs_copy(1, 1).start()

        @pl.when(q == 8)
        def _():
            cycle_terms(up, 0)
            cycle_terms(down, 1)

        @pl.when(q == 9)
        def _():
            cycle_terms(n, 0)
            cycle_terms(n, 1)

        @pl.when(q == 10)
        def _():
            for direction in range(2):
                pltpu.make_async_copy(
                    rbuf.at[direction, 0], rbuf.at[direction, 0], r_rs.at[direction, 0]
                ).wait()
            for ii in range(4):
                part[up, 0, ii] += rbuf[0, 0, ii]
                part[down, 1, ii] += rbuf[1, 0, ii]
            for direction in range(2):
                rs_copy(direction, 2).start()

        @pl.loop(0, 4)
        def _(d):
            def packed(part_of):
                value = ARRIVE[3][part_of]
                for e in range(3):
                    value = jnp.where(d == e, ARRIVE[e][part_of], value)
                return value

            later = chunk(tuple(packed(part_of) for part_of in range(3)), jnp.maximum(q - 1, 0))
            c = jnp.where(q == 0, w * 4 + d, later)
            sibling_in(c)
            pair(c)

    for direction in range(2):
        for item in (1, 2):
            pltpu.make_async_copy(
                rbuf.at[direction, item], rbuf.at[direction, item], r_rs.at[direction, item]
            ).wait()
    lower = lax.broadcasted_iota(jnp.int32, (8, 128), 0) < 4
    for piece in range(2):
        for two in range(2):
            values = [
                part[n, piece, ii]
                + rbuf[0, 2 if piece == 0 else 1, ii]
                + rbuf[1, 1 if piece == 0 else 2, ii]
                for ii in (2 * two, 2 * two + 1)
            ]
            for target in range(16):
                first, second = (v[target * 8:target * 8 + 8, :] for v in values)
                row = target * 64 + (piece * 2 + two) * 8
                zsend[row:row + 8, :] = jnp.where(lower, first, pltpu.roll(second, 4, 0))
                zsend[row + 32:row + 40, :] = jnp.where(lower, pltpu.roll(first, 4, 0), second)

    def back(k):
        target = lax.rem(w + k, wide)
        return pltpu.make_async_remote_copy(
            src_ref=zsend.at[pl.ds(pl.multiple_of(target * 32, 32), 32)],
            dst_ref=zgot.at[pl.ds(mine, 32)],
            send_sem=s_back.at[k], recv_sem=r_back.at[w],
            device_id=(target, n), device_id_type=MESH,
        )

    @pl.loop(1, wide)
    def _(k):
        back(k).start()

    zgot[pl.ds(mine, 32), :] = zsend[pl.ds(mine, 32), :]

    @pl.loop(0, SLOTS)
    def _(s):
        for d in range(4):
            plane_copy(chunk(SEND[d], s), neighbours[d], s_gath.at[d, s]).wait_send()

    @pl.loop(0, 64)
    def _(s):
        plane_copy(0, sib, s_sib.at[s]).wait_send()

    @pl.loop(1, wide)
    def _(k):
        a2a(k).wait_send()

    for item in range(3):
        for direction in range(2):
            y_copy(direction, item).wait_send()
            rs_copy(direction, item).wait_send()

    @pl.loop(1, wide)
    def _(k):
        source = lax.rem(w + k, wide)
        place = zgot.at[pl.ds(pl.multiple_of(source * 32, 32), 32)]
        pltpu.make_async_copy(place, place, r_back.at[source]).wait()

    column = jnp.concatenate([ecol_ref[...], ecol_ref[...]], axis=1)
    base = column - erow_ref[0:1, :] - erow_ref[1:2, :]
    for a in range(4):
        term = jnp.concatenate(
            [zgot[pl.ds(i * 4 + a, 32, stride=32), :] for i in range(8)], axis=0
        ).T
        out_ref[a * 128:(a + 1) * 128, :] = (acc[a * 128:(a + 1) * 128, :] + term) / (
            base + ev_ref[w * 4 + a]
        )

    @pl.loop(1, wide)
    def _(k):
        back(k).wait_send()


def per_device(
    amplitudes, ladder_blocks, ladder_index, cycle_blocks, cycle_index, eps_virt, eps_occ
):
    n = lax.axis_index("narrow")
    virtual = jnp.arange(128, dtype=jnp.int32)
    slots = jnp.arange(16, dtype=jnp.int32)
    match = ladder_index[:, :, None] == virtual[None, None, :]
    inverse = jnp.min(jnp.where(match, slots[None, :, None], 16), axis=1).astype(jnp.int32)
    column = jnp.broadcast_to(eps_virt[:, None], (128, 128))
    here = lax.dynamic_slice_in_dim(eps_occ, n * 8, 8, 0)
    rows = jnp.stack([jnp.repeat(here, 32), jnp.tile(eps_occ, 8)])
    hbm = pl.BlockSpec(memory_space=pl.ANY)
    smem = pl.BlockSpec(memory_space=pltpu.SMEM)
    vmem = pl.BlockSpec(memory_space=pltpu.VMEM)
    dma = pltpu.SemaphoreType.DMA
    return pl.pallas_call(
        kernel,
        name="doubles",
        out_shape=jax.ShapeDtypeStruct((512, 256), F32),
        in_specs=[smem, smem, smem, hbm, hbm, hbm, vmem, vmem],
        out_specs=vmem,
        scratch_shapes=[
            pltpu.VMEM((128, 128, 256), F32),
            pltpu.VMEM((68, 128, 128), BF16),
            pltpu.VMEM((68, 128, 128), BF16),
            pltpu.VMEM((2, 16, 128, 128), F32),
            pltpu.VMEM((32, 4, 128, 128), F32),
            pltpu.VMEM((1024, 128), F32),
            pltpu.VMEM((1024, 128), F32),
            pltpu.VMEM((4, 1024, 128), F32),
            pltpu.VMEM((32, 128, 128), BF16),
            pltpu.VMEM((32, 128, 128), BF16),
            pltpu.VMEM((4, 2, 4, 128, 128), F32),
            pltpu.VMEM((2, 3, 4, 128, 128), F32),
            pltpu.VMEM((1024, 128), F32),
            pltpu.VMEM((1024, 128), F32),
            pltpu.VMEM((512, 256), F32),
            dma, dma((128,)), dma((4, SLOTS)), dma((64,)), dma((2,)), dma,
            dma((32,)), dma((32,)), dma((2, 3)), dma((2, 3)), dma((2, 3)), dma((2, 3)),
            dma((32,)), dma((32,)),
        ],
        compiler_params=pltpu.CompilerParams(
            collective_id=0, has_side_effects=True, vmem_limit_bytes=60 << 20
        ),
    )(
        inverse, cycle_index, eps_virt, amplitudes.reshape(4, 128, 256), ladder_blocks,
        cycle_blocks, column, rows,
    )


def solution(mesh):
    in_specs = (
        P("wide", "narrow"),
        P("wide", None, None, None),
        P("wide", None),
        P(None, "narrow", None, None),
        P(None, "narrow"),
        P(),
        P(),
    )
    return jax.shard_map(
        per_device, mesh=mesh, in_specs=in_specs, out_specs=P("wide", "narrow"), check_vma=False
    )
```

```python
import functools

import jax
import jax.numpy as jnp
from jax import lax
from jax.experimental import pallas as pl
from jax.experimental.pallas import tpu as pltpu
from jax.sharding import PartitionSpec as P

MESH = pl.DeviceIdType.MESH
F32 = jnp.float32
BF16 = jnp.bfloat16
SIDE = 4
SLOTS = 15
AHEAD = 4

X_PLUS = (
    (0, 0, 0), (0, 0, 1), (0, 0, 2), (0, 0, 3), (-1, 0, 0),
    (0, -1, 2), (0, -1, 3), (0, 1, 2), (0, 1, 3), (0, 2, 2), (0, 2, 3),
    (-1, 0, 2), (-1, -1, 2), (-1, 1, 2), (-1, 2, 2),
)
X_MINUS = tuple((-dx, -dz, r ^ 1) for dx, dz, r in X_PLUS)
Z_PLUS = tuple((dz, dx, r ^ 2) for dx, dz, r in X_PLUS)
Z_MINUS = tuple((dz, dx, r ^ 2) for dx, dz, r in X_MINUS)
STREAMS = (X_PLUS, X_MINUS, Z_PLUS, Z_MINUS)
STEPS = ((1, 0), (-1, 0), (0, 1), (0, -1))


def digits(values):
    return sum((value % SIDE) << (2 * position) for position, value in enumerate(values))


SEND = tuple(
    tuple(digits([item[part] for item in stream]) for part in range(3)) for stream in STREAMS
)
ARRIVE = tuple(
    tuple(
        digits([item[part] - (step[part] if part < 2 else 0) for item in stream])
        for part in range(3)
    )
    for stream, step in zip(STREAMS, STEPS)
)


def digit(packed, position):
    return lax.rem(lax.shift_right_logical(packed, 2 * position), SIDE)


def split(value):
    high = value.astype(BF16)
    return high, (value - high.astype(F32)).astype(BF16)


def dot(left, right):
    return jnp.dot(left, right, preferred_element_type=F32)


ROWS = (0, 3, 1, 2)


def kernel(
    lad_idx_ref, cyc_idx_ref, ev_ref, eo_ref, t_ref, lad_ref, cyc_ref, ev_row_ref, out_ref,
    gath, lhi, llo, lstage, cyc, turn, snd, got, thi, tlo, part, rbuf, zsend, zgot, acc,
    inv_v, inv, lad_idx, cyc_idx, ev, eo,
    s_idx, s_inv, s_own, r_gath, s_gath, s_sib, s_lad, s_cyc, s_a2a, r_a2a, s_y, r_y, s_rs, r_rs,
    s_back, r_back,
):
    w = lax.axis_index("wide")
    n = lax.axis_index("narrow")
    core = lax.rem(w, 2)
    chip = w // 2
    x = chip // SIDE
    z = lax.rem(chip, SIDE)
    place_in_row = lax.rem(w, 8)
    sib = w + 1 - 2 * core
    up = lax.rem(n + 1, SIDE)
    down = lax.rem(n + 3, SIDE)
    far = lax.rem(n + 2, SIDE)
    wide = 32
    rows = [lax.rem(x + offset, SIDE) for offset in ROWS]

    def wide_of(dx, dz):
        return (lax.rem(x + dx, SIDE) * SIDE + lax.rem(z + dz, SIDE)) * 2 + core

    neighbours = [wide_of(step[0] % SIDE, step[1] % SIDE) for step in STEPS]

    def chunk(packed, position):
        return wide_of(digit(packed[0], position), digit(packed[1], position)) * 4 + digit(
            packed[2], position
        )

    def plane_copy(c, target, send_sem):
        return pltpu.make_async_remote_copy(
            src_ref=gath.at[c], dst_ref=gath.at[c], send_sem=send_sem, recv_sem=r_gath.at[c],
            device_id=(target, n), device_id_type=MESH,
        )

    def wait_for(place, sem):
        pltpu.make_async_copy(place, place, sem).wait()

    own = pltpu.make_async_copy(t_ref, gath.at[pl.ds(w * 4, 4)], s_own)
    own.start()
    small = [
        pltpu.make_async_copy(source, target, s_idx.at[k])
        for k, (source, target) in enumerate(
            ((lad_idx_ref, lad_idx), (cyc_idx_ref, cyc_idx), (ev_ref, ev), (eo_ref, eo))
        )
    ]
    for copy in small:
        copy.start()

    def lad_load(a):
        return pltpu.make_async_copy(lad_ref.at[a], lstage.at[a % 2], s_lad.at[a % 2])

    lad_load(0).start()
    lad_load(1).start()
    cyc_load = pltpu.make_async_copy(cyc_ref, cyc, s_cyc)
    cyc_load.start()

    barrier = pltpu.get_barrier_semaphore()

    @pl.loop(1, wide)
    def _(k):
        pl.semaphore_signal(
            barrier, inc=1, device_id=(lax.rem(w + k, wide), n), device_id_type=MESH
        )

    for other in (up, down):
        pl.semaphore_signal(barrier, inc=1, device_id=(w, other), device_id_type=MESH)

    own.wait()
    for c in range(4):
        turn[c * 256:(c + 1) * 256, :] = gath[w * 4 + c].T

    @pl.loop(0, wide)
    def _(j):
        for c in range(4):
            row = pl.multiple_of(j * 32 + c * 8, 8)
            snd[pl.ds(row, 8), :] = turn[pl.ds(c * 256 + j, 8, stride=32), :]

    mine = pl.multiple_of(w * 32, 32)
    got[n, pl.ds(mine, 32), :] = snd[pl.ds(mine, 32), :]

    pl.semaphore_wait(barrier, wide + 1)

    for g in range(4):
        row_of = lax.rem(x + (SIDE - ROWS[g]) % SIDE, SIDE)

        @pl.loop(1 if g == 0 else 0, 8)
        def _(m):
            target = row_of * 8 + lax.rem(place_in_row + m, 8)
            pltpu.make_async_remote_copy(
                src_ref=snd.at[pl.ds(pl.multiple_of(target * 32, 32), 32)],
                dst_ref=got.at[n, pl.ds(mine, 32)],
                send_sem=s_a2a, recv_sem=r_a2a.at[g],
                device_id=(target, n), device_id_type=MESH,
            ).start()

    @pl.loop(0, AHEAD)
    def _(s):
        for d in range(4):
            plane_copy(chunk(SEND[d], s), neighbours[d], s_gath.at[d]).start()

    @pl.loop(0, 4)
    def _(r):
        plane_copy(w * 4 + r, sib, s_sib).start()

    for copy in small:
        copy.wait()
    lane = lax.broadcasted_iota(jnp.int32, (8, 128), 1)
    sub = lax.broadcasted_iota(jnp.int32, (8, 128), 0)
    where = jnp.full((8, 128), 16, jnp.int32)
    for a in range(4):
        for s in range(16):
            where = jnp.where((sub == a) & (lane == lad_idx[a, s]), s, where)
    inv_v[...] = where
    inv_copy = pltpu.make_async_copy(inv_v, inv, s_inv)
    inv_copy.start()
    acc[...] = jnp.zeros_like(acc)

    def y_copy(direction, item):
        if item < 4:
            where, g = n, item
        elif direction == 0:
            where, g = down, item - 4
        else:
            where, g = up, item - 2
        place = got.at[where, pl.ds(pl.multiple_of(rows[g] * 256, 256), 256)]
        return pltpu.make_async_remote_copy(
            src_ref=place, dst_ref=place, send_sem=s_y.at[direction],
            recv_sem=r_y.at[direction, item],
            device_id=(w, up if direction == 0 else down), device_id_type=MESH,
        )

    def y_in(item):
        for direction in range(2):
            wait_for(got.at[0, pl.ds(0, 256)], r_y.at[direction, item])

    def spread(slice_of, g):
        row = pl.multiple_of(rows[g] * 32, 32)
        for k in range(8):
            high, low = split(got[slice_of, pl.ds(rows[g] * 256 + k, 32, stride=8), :])
            thi[slice_of * 8 + k, pl.ds(row, 32), :] = high
            tlo[slice_of * 8 + k, pl.ds(row, 32), :] = low

    for g in range(4):
        wait_for(got.at[0, pl.ds(0, 224 if g == 0 else 256)], r_a2a.at[g])
        for direction in range(2):
            y_copy(direction, g).start()
        lad_load(g).wait()

        @pl.loop(0, 16)
        def _(s):
            high, low = split(lstage[g % 2, s])
            lhi[g * 17 + s] = high
            llo[g * 17 + s] = low

        lhi[g * 17 + 16] = jnp.zeros((128, 128), BF16)
        llo[g * 17 + 16] = jnp.zeros((128, 128), BF16)
        if g < 2:
            lad_load(g + 2).start()
    for g in range(4):
        spread(n, g)
    inv_copy.wait()

    def cycle_terms(slice_of, ip):
        @pl.loop(0, 2)
        def _(ii):
            i = slice_of * 8 + ip * 2 + ii
            blocks = [split(cyc[i, s]) for s in range(4)]
            left_high = jnp.concatenate([b[0] for b in blocks], axis=1)
            left_low = jnp.concatenate([b[1] for b in blocks], axis=1)
            listed = [cyc_idx[s, i] for s in range(4)]
            right_high = jnp.concatenate([thi[k] for k in listed], axis=0)
            right_low = jnp.concatenate([tlo[k] for k in listed], axis=0)
            part[slice_of, ip, ii] = (
                dot(left_high, right_high) + dot(left_low, right_high) + dot(left_high, right_low)
            )

    flip = (0, 2)

    def rs_copy(direction, slot):
        near = up if direction == 0 else down
        target, ip = ((far, 0), (far, 1), (near, 2), (near, 0), (near, 3), (near, 1))[slot]
        return pltpu.make_async_remote_copy(
            src_ref=part.at[target, ip ^ flip[direction]], dst_ref=rbuf.at[direction, slot],
            send_sem=s_rs.at[direction], recv_sem=r_rs.at[direction, slot],
            device_id=(w, near), device_id_type=MESH,
        )

    def rs_send(slot):
        for direction in range(2):
            rs_copy(direction, slot).start()

    def rs_in(slot):
        for direction in range(2):
            wait_for(rbuf.at[direction, slot], r_rs.at[direction, slot])

    def merge(slot):
        rs_in(slot)
        part[up, slot] += rbuf[0, slot]
        part[down, slot ^ 2] += rbuf[1, slot]

    lower = lax.broadcasted_iota(jnp.int32, (8, 128), 0) < 4

    def give_back(half):
        for item in range(2):
            ip = half + 2 * item
            slots = {0: (3, 2), 2: (2, 3), 1: (5, 4), 3: (4, 5)}[ip]
            values = [
                part[n, ip, ii] + rbuf[0, slots[0], ii] + rbuf[1, slots[1], ii] for ii in range(2)
            ]
            for target in range(16):
                first, second = (v[target * 8:target * 8 + 8, :] for v in values)
                row = target * 32 + item * 8
                zsend[half, row:row + 8, :] = jnp.where(lower, first, pltpu.roll(second, 4, 0))
                zsend[half, row + 16:row + 24, :] = jnp.where(
                    lower, pltpu.roll(first, 4, 0), second
                )

        here = pl.multiple_of(w * 16, 16)

        @pl.loop(1, wide)
        def _(k):
            target = lax.rem(w + k, wide)
            pltpu.make_async_remote_copy(
                src_ref=zsend.at[half, pl.ds(pl.multiple_of(target * 16, 16), 16)],
                dst_ref=zgot.at[half, pl.ds(here, 16)],
                send_sem=s_back.at[half], recv_sem=r_back.at[half],
                device_id=(target, n), device_id_type=MESH,
            ).start()

        zgot[half, pl.ds(here, 16), :] = zsend[half, pl.ds(here, 16), :]

    def pair(c):
        other = c + 4 - 8 * core
        high_0, low_0 = split(gath[c])
        high_1, low_1 = split(gath[other])
        high = jnp.concatenate([high_0, high_1], axis=0)
        low = jnp.concatenate([low_0, low_1], axis=0)

        def taken(table):
            return jnp.concatenate(
                [
                    jnp.concatenate(
                        [table[a * 17 + inv[a, c]], table[a * 17 + inv[a, other]]], axis=1
                    )
                    for a in range(4)
                ],
                axis=0,
            )

        left_high, left_low = taken(lhi), taken(llo)
        acc[...] += dot(left_high, high) + dot(left_low, high) + dot(left_high, low)

    @pl.loop(0, SLOTS + 1)
    def _(q):
        @pl.when(q < SLOTS)
        def _():
            for d in range(4):
                c = chunk(ARRIVE[d], q)
                wait_for(gath.at[c], r_gath.at[c])
                plane_copy(c, sib, s_sib).start()

        @pl.when(q < SLOTS - AHEAD)
        def _():
            for d in range(4):
                plane_copy(chunk(SEND[d], q + AHEAD), neighbours[d], s_gath.at[d]).start()

        @pl.when(q == 0)
        def _():
            for item in range(2):
                y_in(item)
                y_copy(0, 4 + item).start()
                spread(down, item)
                spread(up, item)

        @pl.when(q == 1)
        def _():
            y_in(2)
            y_copy(1, 4).start()
            spread(down, 2)
            spread(up, 2)

        @pl.when(q == 2)
        def _():
            y_in(3)
            y_copy(1, 5).start()
            spread(down, 3)
            spread(up, 3)

        @pl.when(q == 3)
        def _():
            y_in(4)
            spread(far, 0)
            spread(far, 2)

        @pl.when(q == 4)
        def _():
            cyc_load.wait()
            y_in(5)
            spread(far, 1)
            spread(far, 3)
            cycle_terms(far, 0)
            rs_copy(0, 0).start()
            cycle_terms(far, 2)
            rs_copy(1, 0).start()

        @pl.when(q == 5)
        def _():
            cycle_terms(far, 1)
            cycle_terms(far, 3)
            rs_send(1)
            cycle_terms(up, 2)
            cycle_terms(down, 0)
            rs_send(2)

        @pl.when(q == 6)
        def _():
            cycle_terms(up, 0)
            cycle_terms(down, 2)
            merge(0)
            rs_send(3)

        @pl.when(q == 7)
        def _():
            cycle_terms(up, 3)
            cycle_terms(down, 1)
            rs_send(4)

        @pl.when(q == 8)
        def _():
            cycle_terms(up, 1)
            cycle_terms(down, 3)
            merge(1)
            rs_send(5)

        @pl.when(q == 9)
        def _():
            for ip in range(4):
                cycle_terms(n, ip)

        @pl.when(q == 10)
        def _():
            rs_in(2)
            rs_in(3)
            give_back(0)

        @pl.when(q == 12)
        def _():
            rs_in(4)
            rs_in(5)
            give_back(1)

        @pl.loop(0, 4)
        def _(d):
            def packed(part_of):
                value = ARRIVE[3][part_of]
                for e in range(3):
                    value = jnp.where(d == e, ARRIVE[e][part_of], value)
                return value

            later = chunk(tuple(packed(part_of) for part_of in range(3)), jnp.maximum(q - 1, 0))
            c = jnp.where(q == 0, w * 4 + d, later)
            other = c + 4 - 8 * core
            wait_for(gath.at[other], r_gath.at[other])
            pair(c)

    column = jnp.broadcast_to(ev_row_ref[...], (128, 128)).T
    lanes = lax.broadcasted_iota(jnp.int32, (8, 256), 1)
    first, second = lanes // 32, lax.rem(lanes, 32)
    row_i = jnp.full((8, 256), eo[n * 8], F32)
    for i in range(1, 8):
        row_i = jnp.where(first == i, eo[n * 8 + i], row_i)
    row_j = jnp.full((8, 256), eo[0], F32)
    for j in range(1, 32):
        row_j = jnp.where(second == j, eo[j], row_j)
    base = jnp.concatenate([column, column], axis=1)
    less_i, less_j = row_i[0:1, :], row_j[0:1, :]

    for d in range(4):
        wait_for(gath.at[pl.ds(0, SLOTS)], s_gath.at[d])
    wait_for(gath.at[pl.ds(0, 64)], s_sib)
    wait_for(snd.at[pl.ds(0, 992)], s_a2a)
    for direction in range(2):
        wait_for(rbuf.at[direction], s_rs.at[direction])
        wait_for(rbuf.at[direction], s_y.at[direction])
    for half in range(2):
        wait_for(zgot.at[half, pl.ds(0, 496)], r_back.at[half])

    for a in range(4):
        term = jnp.concatenate(
            [
                zgot[i // 2 % 2, pl.ds(i // 4 * 8 + i % 2 * 4 + a, 32, stride=16), :]
                for i in range(8)
            ],
            axis=0,
        ).T
        energy = (ev[w * 4 + a] + base) - less_i - less_j
        out_ref[a * 128:(a + 1) * 128, :] = (acc[a * 128:(a + 1) * 128, :] + term) / energy

    for half in range(2):
        wait_for(zsend.at[half, pl.ds(0, 496)], s_back.at[half])


def per_device(
    amplitudes, ladder_blocks, ladder_index, cycle_blocks, cycle_index, eps_virt, eps_occ
):
    hbm = pl.BlockSpec(memory_space=pl.ANY)
    vmem = pl.BlockSpec(memory_space=pltpu.VMEM)
    dma = pltpu.SemaphoreType.DMA
    return pl.pallas_call(
        kernel,
        name="doubles",
        out_shape=jax.ShapeDtypeStruct((512, 256), F32),
        in_specs=[hbm, hbm, hbm, hbm, hbm, hbm, hbm, vmem],
        out_specs=vmem,
        scratch_shapes=[
            pltpu.VMEM((128, 128, 256), F32),
            pltpu.VMEM((68, 128, 128), BF16),
            pltpu.VMEM((68, 128, 128), BF16),
            pltpu.VMEM((2, 16, 128, 128), F32),
            pltpu.VMEM((32, 4, 128, 128), F32),
            pltpu.VMEM((1024, 128), F32),
            pltpu.VMEM((1024, 128), F32),
            pltpu.VMEM((4, 1024, 128), F32),
            pltpu.VMEM((32, 128, 128), BF16),
            pltpu.VMEM((32, 128, 128), BF16),
            pltpu.VMEM((4, 4, 2, 128, 128), F32),
            pltpu.VMEM((2, 6, 2, 128, 128), F32),
            pltpu.VMEM((2, 512, 128), F32),
            pltpu.VMEM((2, 512, 128), F32),
            pltpu.VMEM((512, 256), F32),
            pltpu.VMEM((8, 128), jnp.int32),
            pltpu.SMEM((8, 128), jnp.int32),
            pltpu.SMEM((4, 16), jnp.int32),
            pltpu.SMEM((4, 32), jnp.int32),
            pltpu.SMEM((128,), F32),
            pltpu.SMEM((32,), F32),
            dma((4,)), dma, dma, dma((128,)), dma((4,)), dma, dma((2,)), dma,
            dma, dma((4,)), dma((2,)), dma((2, 6)), dma((2,)), dma((2, 6)),
            dma((2,)), dma((2,)),
        ],
        compiler_params=pltpu.CompilerParams(
            collective_id=0, has_side_effects=True, vmem_limit_bytes=60 << 20
        ),
    )(
        ladder_index, cycle_index.T, eps_virt, eps_occ, amplitudes.reshape(4, 128, 256),
        ladder_blocks, cycle_blocks, eps_virt[None, :],
    )


def solution(mesh):
    in_specs = (
        P("wide", "narrow"),
        P("wide", None, None, None),
        P("wide", None),
        P(None, "narrow", None, None),
        P(None, "narrow"),
        P(),
        P(),
    )
    return jax.shard_map(
        per_device, mesh=mesh, in_specs=in_specs, out_specs=P("wide", "narrow"), check_vma=False
    )
```

```python
import functools

import jax
import jax.numpy as jnp
from jax import lax
from jax.experimental import pallas as pl
from jax.experimental.pallas import tpu as pltpu
from jax.sharding import PartitionSpec as P

MESH = pl.DeviceIdType.MESH
F32 = jnp.float32
BF16 = jnp.bfloat16
SIDE = 4
SLOTS = 15
AHEAD = 5

X_PLUS = (
    (0, 0, 0), (0, 0, 1), (0, 0, 2), (0, 0, 3), (-1, 0, 0),
    (0, -1, 2), (0, -1, 3), (0, 1, 2), (0, 1, 3), (0, 2, 2), (0, 2, 3),
    (-1, 0, 2), (-1, -1, 2), (-1, 1, 2), (-1, 2, 2),
)
X_MINUS = tuple((-dx, -dz, r ^ 1) for dx, dz, r in X_PLUS)
Z_PLUS = tuple((dz, dx, r ^ 2) for dx, dz, r in X_PLUS)
Z_MINUS = tuple((dz, dx, r ^ 2) for dx, dz, r in X_MINUS)
STREAMS = (X_PLUS, X_MINUS, Z_PLUS, Z_MINUS)
STEPS = ((1, 0), (-1, 0), (0, 1), (0, -1))


def digits(values):
    return sum((value % SIDE) << (2 * position) for position, value in enumerate(values))


SEND = tuple(
    tuple(digits([item[part] for item in stream]) for part in range(3)) for stream in STREAMS
)
ARRIVE = tuple(
    tuple(
        digits([item[part] - (step[part] if part < 2 else 0) for item in stream])
        for part in range(3)
    )
    for stream, step in zip(STREAMS, STEPS)
)


def digit(packed, position):
    return lax.rem(lax.shift_right_logical(packed, 2 * position), SIDE)


def split(value):
    high = value.astype(BF16)
    return high, (value - high.astype(F32)).astype(BF16)


def dot(left, right):
    return jnp.dot(left, right, preferred_element_type=F32)


ROWS = (0, 3, 1, 2)


def kernel(
    lad_idx_ref, cyc_idx_ref, ev_ref, eo_ref, t_ref, lad_ref, cyc_ref, ev_row_ref, out_ref,
    gath, lhi, llo, lstage, cyc, turn, snd, got, thi, tlo, part, rbuf, zsend, zgot, acc,
    inv_v, inv, lad_idx, cyc_idx, ev, eo, ev_row, den, out_v,
    s_idx, s_inv, s_own, r_gath, s_gath, s_sib, s_lad, s_cyc, s_a2a, r_a2a, s_y, r_y, s_rs, r_rs,
    s_back, r_back, s_out,
):
    w = lax.axis_index("wide")
    n = lax.axis_index("narrow")
    core = lax.rem(w, 2)
    chip = w // 2
    x = chip // SIDE
    z = lax.rem(chip, SIDE)
    place_in_row = lax.rem(w, 8)
    sib = w + 1 - 2 * core
    up = lax.rem(n + 1, SIDE)
    down = lax.rem(n + 3, SIDE)
    far = lax.rem(n + 2, SIDE)
    wide = 32
    rows = [lax.rem(x + offset, SIDE) for offset in ROWS]

    def wide_of(dx, dz):
        return (lax.rem(x + dx, SIDE) * SIDE + lax.rem(z + dz, SIDE)) * 2 + core

    neighbours = [wide_of(step[0] % SIDE, step[1] % SIDE) for step in STEPS]

    def chunk(packed, position):
        return wide_of(digit(packed[0], position), digit(packed[1], position)) * 4 + digit(
            packed[2], position
        )

    def plane_copy(c, target, send_sem):
        return pltpu.make_async_remote_copy(
            src_ref=gath.at[c], dst_ref=gath.at[c], send_sem=send_sem, recv_sem=r_gath.at[c],
            device_id=(target, n), device_id_type=MESH,
        )

    def wait_for(place, sem):
        pltpu.make_async_copy(place, place, sem).wait()

    barrier = pltpu.get_barrier_semaphore()

    @pl.loop(1, wide)
    def _(k):
        pl.semaphore_signal(
            barrier, inc=1, device_id=(lax.rem(w + k, wide), n), device_id_type=MESH
        )

    for other in (up, down):
        pl.semaphore_signal(barrier, inc=1, device_id=(w, other), device_id_type=MESH)

    own = pltpu.make_async_copy(t_ref, gath.at[pl.ds(w * 4, 4)], s_own)
    own.start()
    small = [
        pltpu.make_async_copy(source, target, s_idx.at[k])
        for k, (source, target) in enumerate(
            (
                (lad_idx_ref, lad_idx), (cyc_idx_ref, cyc_idx), (ev_ref, ev), (eo_ref, eo),
                (ev_row_ref, ev_row),
            )
        )
    ]
    for copy in small:
        copy.start()

    def lad_load(a):
        return pltpu.make_async_copy(lad_ref.at[a], lstage.at[a % 2], s_lad.at[a % 2])

    lad_load(0).start()
    lad_load(1).start()
    cyc_load = pltpu.make_async_copy(cyc_ref, cyc, s_cyc)
    cyc_load.start()

    own.wait()
    for c in range(4):
        turn[c * 256:(c + 1) * 256, :] = gath[w * 4 + c].T

    @pl.loop(0, wide)
    def _(j):
        for c in range(4):
            row = pl.multiple_of(j * 32 + c * 8, 8)
            snd[pl.ds(row, 8), :] = turn[pl.ds(c * 256 + j, 8, stride=32), :]

    mine = pl.multiple_of(w * 32, 32)
    got[n, pl.ds(mine, 32), :] = snd[pl.ds(mine, 32), :]

    def plane_send(s):
        for d in range(4):
            plane_copy(chunk(SEND[d], s), neighbours[d], s_gath.at[d]).start()

    def give_row(g):
        row_of = lax.rem(x + (SIDE - ROWS[g]) % SIDE, SIDE)

        @pl.loop(1 if g == 0 else 0, 8)
        def _(m):
            target = row_of * 8 + lax.rem(place_in_row + m, 8)
            pltpu.make_async_remote_copy(
                src_ref=snd.at[pl.ds(pl.multiple_of(target * 32, 32), 32)],
                dst_ref=got.at[n, pl.ds(mine, 32)],
                send_sem=s_a2a, recv_sem=r_a2a.at[g],
                device_id=(target, n), device_id_type=MESH,
            ).start()

    pl.semaphore_wait(barrier, wide + 1)
    for g in range(4):
        give_row(g)

    @pl.loop(0, 4)
    def _(r):
        plane_copy(w * 4 + r, sib, s_sib).start()

    for copy in small:
        copy.wait()
    lane = lax.broadcasted_iota(jnp.int32, (8, 128), 1)
    sub = lax.broadcasted_iota(jnp.int32, (8, 128), 0)
    where = jnp.full((8, 128), 16, jnp.int32)
    for a in range(4):
        for s in range(16):
            where = jnp.where((sub == a) & (lane == lad_idx[a, s]), s, where)
    inv_v[...] = where
    inv_copy = pltpu.make_async_copy(inv_v, inv, s_inv)
    inv_copy.start()
    acc[...] = jnp.zeros_like(acc)

    def y_copy(direction, item):
        if item < 4:
            where, g = n, item
        elif direction == 0:
            where, g = down, item - 4
        else:
            where, g = up, item - 2
        place = got.at[where, pl.ds(pl.multiple_of(rows[g] * 256, 256), 256)]
        return pltpu.make_async_remote_copy(
            src_ref=place, dst_ref=place, send_sem=s_y.at[direction],
            recv_sem=r_y.at[direction, item],
            device_id=(w, up if direction == 0 else down), device_id_type=MESH,
        )

    def y_in(item):
        for direction in range(2):
            wait_for(got.at[0, pl.ds(0, 256)], r_y.at[direction, item])

    def spread(slice_of, g):
        row = pl.multiple_of(rows[g] * 32, 32)
        for k in range(8):
            high, low = split(got[slice_of, pl.ds(rows[g] * 256 + k, 32, stride=8), :])
            thi[slice_of * 8 + k, pl.ds(row, 32), :] = high
            tlo[slice_of * 8 + k, pl.ds(row, 32), :] = low

    for g in range(4):
        wait_for(got.at[0, pl.ds(0, 224 if g == 0 else 256)], r_a2a.at[g])
        for direction in range(2):
            y_copy(direction, g).start()
        plane_send(g)
        lad_load(g).wait()

        @pl.loop(0, 16)
        def _(s):
            high, low = split(lstage[g % 2, s])
            lhi[g * 17 + s] = high
            llo[g * 17 + s] = low

        lhi[g * 17 + 16] = jnp.zeros((128, 128), BF16)
        llo[g * 17 + 16] = jnp.zeros((128, 128), BF16)
        if g < 2:
            lad_load(g + 2).start()
    for g in range(4):
        spread(n, g)
    inv_copy.wait()

    column = jnp.broadcast_to(ev_row[...], (128, 128)).T
    lanes = lax.broadcasted_iota(jnp.int32, (8, 256), 1)
    first, second = lanes // 32, lax.rem(lanes, 32)
    row_i = jnp.full((8, 256), eo[n * 8], F32)
    for i in range(1, 8):
        row_i = jnp.where(first == i, eo[n * 8 + i], row_i)
    row_j = jnp.full((8, 256), eo[0], F32)
    for j in range(1, 32):
        row_j = jnp.where(second == j, eo[j], row_j)
    base = jnp.concatenate([column, column], axis=1)
    less_i, less_j = row_i[0:1, :], row_j[0:1, :]

    for a in range(4):
        den[a * 128:(a + 1) * 128, :] = (ev[w * 4 + a] + base) - less_i - less_j

    def cycle_terms(slice_of, ip):
        @pl.loop(0, 2)
        def _(ii):
            i = slice_of * 8 + ip * 2 + ii
            blocks = [split(cyc[i, s]) for s in range(4)]
            left_high = jnp.concatenate([b[0] for b in blocks], axis=1)
            left_low = jnp.concatenate([b[1] for b in blocks], axis=1)
            listed = [cyc_idx[s, i] for s in range(4)]
            right_high = jnp.concatenate([thi[k] for k in listed], axis=0)
            right_low = jnp.concatenate([tlo[k] for k in listed], axis=0)
            part[slice_of, ip, ii] = (
                dot(left_high, right_high) + dot(left_low, right_high) + dot(left_high, right_low)
            )

    flip = (0, 2)

    def rs_copy(direction, slot):
        near = up if direction == 0 else down
        target, ip = ((far, 0), (far, 1), (near, 2), (near, 0), (near, 3), (near, 1))[slot]
        return pltpu.make_async_remote_copy(
            src_ref=part.at[target, ip ^ flip[direction]], dst_ref=rbuf.at[direction, slot],
            send_sem=s_rs.at[direction], recv_sem=r_rs.at[direction, slot],
            device_id=(w, near), device_id_type=MESH,
        )

    def rs_send(slot):
        for direction in range(2):
            rs_copy(direction, slot).start()

    def rs_in(slot):
        for direction in range(2):
            wait_for(rbuf.at[direction, slot], r_rs.at[direction, slot])

    def merge(slot):
        rs_in(slot)
        part[up, slot] += rbuf[0, slot]
        part[down, slot ^ 2] += rbuf[1, slot]

    lower = lax.broadcasted_iota(jnp.int32, (8, 128), 0) < 4

    def give_back(half):
        for item in range(2):
            ip = half + 2 * item
            slots = {0: (3, 2), 2: (2, 3), 1: (5, 4), 3: (4, 5)}[ip]
            values = [
                part[n, ip, ii] + rbuf[0, slots[0], ii] + rbuf[1, slots[1], ii] for ii in range(2)
            ]
            for target in range(16):
                first, second = (v[target * 8:target * 8 + 8, :] for v in values)
                row = target * 32 + item * 8
                zsend[half, row:row + 8, :] = jnp.where(lower, first, pltpu.roll(second, 4, 0))
                zsend[half, row + 16:row + 24, :] = jnp.where(
                    lower, pltpu.roll(first, 4, 0), second
                )

        here = pl.multiple_of(w * 16, 16)

        @pl.loop(1, wide)
        def _(k):
            target = lax.rem(w + k, wide)
            pltpu.make_async_remote_copy(
                src_ref=zsend.at[half, pl.ds(pl.multiple_of(target * 16, 16), 16)],
                dst_ref=zgot.at[half, pl.ds(here, 16)],
                send_sem=s_back.at[half], recv_sem=r_back.at[half],
                device_id=(target, n), device_id_type=MESH,
            ).start()

        zgot[half, pl.ds(here, 16), :] = zsend[half, pl.ds(here, 16), :]

    def pair(c):
        other = c + 4 - 8 * core
        high_0, low_0 = split(gath[c])
        high_1, low_1 = split(gath[other])
        high = jnp.concatenate([high_0, high_1], axis=0)
        low = jnp.concatenate([low_0, low_1], axis=0)

        def taken(table):
            return jnp.concatenate(
                [
                    jnp.concatenate(
                        [table[a * 17 + inv[a, c]], table[a * 17 + inv[a, other]]], axis=1
                    )
                    for a in range(4)
                ],
                axis=0,
            )

        left_high, left_low = taken(lhi), taken(llo)
        acc[...] += dot(left_high, high) + dot(left_low, high) + dot(left_high, low)

    def pairs_of(q):
        @pl.loop(0, 4)
        def _(d):
            def packed(part_of):
                value = ARRIVE[3][part_of]
                for e in range(3):
                    value = jnp.where(d == e, ARRIVE[e][part_of], value)
                return value

            later = chunk(tuple(packed(part_of) for part_of in range(3)), jnp.maximum(q - 1, 0))
            c = jnp.where(q == 0, w * 4 + d, later)
            other = c + 4 - 8 * core
            wait_for(gath.at[other], r_gath.at[other])
            pair(c)

    @pl.loop(0, SLOTS)
    def _(q):
        for d in range(4):
            c = chunk(ARRIVE[d], q)
            wait_for(gath.at[c], r_gath.at[c])
            plane_copy(c, sib, s_sib).start()

        @pl.when(q == 0)
        def _():
            plane_send(AHEAD - 1)

        @pl.when(q < SLOTS - AHEAD)
        def _():
            plane_send(q + AHEAD)

        @pl.when(q == 0)
        def _():
            for item in range(2):
                y_in(item)
                y_copy(0, 4 + item).start()
                spread(down, item)
                spread(up, item)

        @pl.when(q == 1)
        def _():
            y_in(2)
            y_copy(1, 4).start()
            spread(down, 2)
            spread(up, 2)

        @pl.when(q == 2)
        def _():
            y_in(3)
            y_copy(1, 5).start()
            spread(down, 3)
            spread(up, 3)

        @pl.when(q == 3)
        def _():
            y_in(4)
            spread(far, 0)
            spread(far, 2)

        @pl.when(q == 5)
        def _():
            cyc_load.wait()
            y_in(5)
            spread(far, 1)
            spread(far, 3)
            cycle_terms(far, 0)
            rs_copy(0, 0).start()
            cycle_terms(far, 2)
            rs_copy(1, 0).start()

        @pl.when(q == 6)
        def _():
            cycle_terms(far, 1)
            cycle_terms(far, 3)
            rs_send(1)
            cycle_terms(up, 2)
            cycle_terms(down, 0)
            rs_send(2)

        @pl.when(q == 7)
        def _():
            cycle_terms(up, 0)
            cycle_terms(down, 2)
            merge(0)
            rs_send(3)

        @pl.when(q == 8)
        def _():
            cycle_terms(up, 3)
            cycle_terms(down, 1)
            rs_send(4)

        @pl.when(q == 9)
        def _():
            cycle_terms(up, 1)
            cycle_terms(down, 3)
            merge(1)
            rs_send(5)

        @pl.when(q == 10)
        def _():
            for ip in range(4):
                cycle_terms(n, ip)

        @pl.when(q == 11)
        def _():
            rs_in(2)
            rs_in(3)
            give_back(0)

        @pl.when(q == 13)
        def _():
            rs_in(4)
            rs_in(5)
            give_back(1)

        pairs_of(q)

    pairs_of(SLOTS)

    for d in range(4):
        wait_for(gath.at[pl.ds(0, SLOTS)], s_gath.at[d])
    wait_for(gath.at[pl.ds(0, 64)], s_sib)
    wait_for(snd.at[pl.ds(0, 992)], s_a2a)
    for direction in range(2):
        wait_for(rbuf.at[direction], s_rs.at[direction])
        wait_for(rbuf.at[direction], s_y.at[direction])
    for half in range(2):
        wait_for(zgot.at[half, pl.ds(0, 496)], r_back.at[half])

    for a in range(4):
        term = jnp.concatenate(
            [
                zgot[i // 2 % 2, pl.ds(i // 4 * 8 + i % 2 * 4 + a, 32, stride=16), :]
                for i in range(8)
            ],
            axis=0,
        ).T
        here = slice(a * 128, (a + 1) * 128)
        out_v[here, :] = (acc[here, :] + term) / den[here, :]
        pltpu.make_async_copy(out_v.at[here], out_ref.at[here], s_out.at[a]).start()

    for half in range(2):
        wait_for(zsend.at[half, pl.ds(0, 496)], s_back.at[half])
    for a in range(4):
        here = slice(a * 128, (a + 1) * 128)
        pltpu.make_async_copy(out_v.at[here], out_ref.at[here], s_out.at[a]).wait()


def per_device(
    amplitudes, ladder_blocks, ladder_index, cycle_blocks, cycle_index, eps_virt, eps_occ
):
    hbm = pl.BlockSpec(memory_space=pl.ANY)
    dma = pltpu.SemaphoreType.DMA
    return pl.pallas_call(
        kernel,
        name="doubles",
        out_shape=jax.ShapeDtypeStruct((512, 256), F32),
        in_specs=[hbm] * 8,
        out_specs=hbm,
        scratch_shapes=[
            pltpu.VMEM((128, 128, 256), F32),
            pltpu.VMEM((68, 128, 128), BF16),
            pltpu.VMEM((68, 128, 128), BF16),
            pltpu.VMEM((2, 16, 128, 128), F32),
            pltpu.VMEM((32, 4, 128, 128), F32),
            pltpu.VMEM((1024, 128), F32),
            pltpu.VMEM((1024, 128), F32),
            pltpu.VMEM((4, 1024, 128), F32),
            pltpu.VMEM((32, 128, 128), BF16),
            pltpu.VMEM((32, 128, 128), BF16),
            pltpu.VMEM((4, 4, 2, 128, 128), F32),
            pltpu.VMEM((2, 6, 2, 128, 128), F32),
            pltpu.VMEM((2, 512, 128), F32),
            pltpu.VMEM((2, 512, 128), F32),
            pltpu.VMEM((512, 256), F32),
            pltpu.VMEM((8, 128), jnp.int32),
            pltpu.SMEM((8, 128), jnp.int32),
            pltpu.SMEM((4, 16), jnp.int32),
            pltpu.SMEM((4, 32), jnp.int32),
            pltpu.SMEM((128,), F32),
            pltpu.SMEM((32,), F32),
            pltpu.VMEM((1, 128), F32),
            pltpu.VMEM((512, 256), F32),
            pltpu.VMEM((512, 256), F32),
            dma((5,)), dma, dma, dma((128,)), dma((4,)), dma, dma((2,)), dma,
            dma, dma((4,)), dma((2,)), dma((2, 6)), dma((2,)), dma((2, 6)),
            dma((2,)), dma((2,)), dma((4,)),
        ],
        compiler_params=pltpu.CompilerParams(
            collective_id=0, has_side_effects=True, vmem_limit_bytes=60 << 20
        ),
    )(
        ladder_index, cycle_index.T, eps_virt, eps_occ, amplitudes.reshape(4, 128, 256),
        ladder_blocks, cycle_blocks, eps_virt[None, :],
    )


def solution(mesh):
    in_specs = (
        P("wide", "narrow"),
        P("wide", None, None, None),
        P("wide", None),
        P(None, "narrow", None, None),
        P(None, "narrow"),
        P(),
        P(),
    )
    return jax.shard_map(
        per_device, mesh=mesh, in_specs=in_specs, out_specs=P("wide", "narrow"), check_vma=False
    )
```

```python
import functools

import jax
import jax.numpy as jnp
from jax import lax
from jax.experimental import pallas as pl
from jax.experimental.pallas import tpu as pltpu
from jax.sharding import PartitionSpec as P

MESH = pl.DeviceIdType.MESH
F32 = jnp.float32
BF16 = jnp.bfloat16
SIDE = 4
SLOTS = 15
AHEAD = 5

X_PLUS = (
    (0, 0, 0), (0, 0, 1), (0, 0, 2), (0, 0, 3), (-1, 0, 0),
    (0, -1, 2), (0, -1, 3), (0, 1, 2), (0, 1, 3), (0, 2, 2), (0, 2, 3),
    (-1, 0, 2), (-1, -1, 2), (-1, 1, 2), (-1, 2, 2),
)
X_MINUS = tuple((-dx, -dz, r ^ 1) for dx, dz, r in X_PLUS)
Z_PLUS = tuple((dz, dx, r ^ 2) for dx, dz, r in X_PLUS)
Z_MINUS = tuple((dz, dx, r ^ 2) for dx, dz, r in X_MINUS)
STREAMS = (X_PLUS, X_MINUS, Z_PLUS, Z_MINUS)
STEPS = ((1, 0), (-1, 0), (0, 1), (0, -1))


def digits(values):
    return sum((value % SIDE) << (2 * position) for position, value in enumerate(values))


SEND = tuple(
    tuple(digits([item[part] for item in stream]) for part in range(3)) for stream in STREAMS
)
ARRIVE = tuple(
    tuple(
        digits([item[part] - (step[part] if part < 2 else 0) for item in stream])
        for part in range(3)
    )
    for stream, step in zip(STREAMS, STEPS)
)


def digit(packed, position):
    return lax.rem(lax.shift_right_logical(packed, 2 * position), SIDE)


def split(value):
    high = value.astype(BF16)
    return high, (value - high.astype(F32)).astype(BF16)


def dot(left, right):
    return jnp.dot(left, right, preferred_element_type=F32)


ROWS = (0, 3, 1, 2)


def kernel(
    lad_idx_ref, cyc_idx_ref, ev_ref, eo_ref, t_ref, lad_ref, cyc_ref, ev_row_ref, out_ref,
    gath, lhi, llo, lstage, cyc, turn, snd, got, thi, tlo, part, rbuf, zsend, zgot, acc,
    inv_v, inv, lad_idx, cyc_idx, ev, eo, ev_row, den, out_v,
    s_idx, s_inv, s_own, r_gath, s_gath, s_sib, s_lad, s_cyc, s_a2a, r_a2a, s_y, r_y, s_rs, r_rs,
    s_back, r_back, s_out,
):
    w = lax.axis_index("wide")
    n = lax.axis_index("narrow")
    core = lax.rem(w, 2)
    chip = w // 2
    x = chip // SIDE
    z = lax.rem(chip, SIDE)
    place_in_row = lax.rem(w, 8)
    sib = w + 1 - 2 * core
    up = lax.rem(n + 1, SIDE)
    down = lax.rem(n + 3, SIDE)
    far = lax.rem(n + 2, SIDE)
    wide = 32
    rows = [lax.rem(x + offset, SIDE) for offset in ROWS]

    def wide_of(dx, dz):
        return (lax.rem(x + dx, SIDE) * SIDE + lax.rem(z + dz, SIDE)) * 2 + core

    neighbours = [wide_of(step[0] % SIDE, step[1] % SIDE) for step in STEPS]

    def chunk(packed, position):
        return wide_of(digit(packed[0], position), digit(packed[1], position)) * 4 + digit(
            packed[2], position
        )

    def plane_copy(c, target, send_sem):
        return pltpu.make_async_remote_copy(
            src_ref=gath.at[c], dst_ref=gath.at[c], send_sem=send_sem, recv_sem=r_gath.at[c],
            device_id=(target, n), device_id_type=MESH,
        )

    def wait_for(place, sem):
        pltpu.make_async_copy(place, place, sem).wait()

    barrier = pltpu.get_barrier_semaphore()

    @pl.loop(1, wide)
    def _(k):
        pl.semaphore_signal(
            barrier, inc=1, device_id=(lax.rem(w + k, wide), n), device_id_type=MESH
        )

    for other in (up, down):
        pl.semaphore_signal(barrier, inc=1, device_id=(w, other), device_id_type=MESH)

    own = pltpu.make_async_copy(t_ref, gath.at[pl.ds(w * 4, 4)], s_own)
    own.start()
    small = [
        pltpu.make_async_copy(source, target, s_idx.at[k])
        for k, (source, target) in enumerate(
            (
                (lad_idx_ref, lad_idx), (cyc_idx_ref, cyc_idx), (ev_ref, ev), (eo_ref, eo),
                (ev_row_ref, ev_row),
            )
        )
    ]
    for copy in small:
        copy.start()

    def lad_load(a):
        return pltpu.make_async_copy(lad_ref.at[a], lstage.at[a % 2], s_lad.at[a % 2])

    lad_load(0).start()
    lad_load(1).start()
    cyc_load = pltpu.make_async_copy(cyc_ref, cyc, s_cyc)
    cyc_load.start()

    own.wait()
    for c in range(4):
        turn[c * 256:(c + 1) * 256, :] = gath[w * 4 + c].T

    @pl.loop(0, wide)
    def _(j):
        for c in range(4):
            row = pl.multiple_of(j * 32 + c * 8, 8)
            snd[pl.ds(row, 8), :] = turn[pl.ds(c * 256 + j, 8, stride=32), :]

    mine = pl.multiple_of(w * 32, 32)
    got[n, pl.ds(mine, 32), :] = snd[pl.ds(mine, 32), :]

    def plane_send(s):
        for d in range(4):
            plane_copy(chunk(SEND[d], s), neighbours[d], s_gath.at[d]).start()

    pl.semaphore_wait(barrier, wide + 1)

    @pl.loop(0, 8)
    def _(m):
        for g in (0, 1, 2, 3):
            @pl.when((lax.rem(m * 3, 8) > 0) | (g > 0))
            def _():
                row_of = lax.rem(x + (SIDE - ROWS[g]) % SIDE, SIDE)
                target = row_of * 8 + lax.rem(place_in_row + lax.rem(m * 3, 8), 8)
                pltpu.make_async_remote_copy(
                    src_ref=snd.at[pl.ds(pl.multiple_of(target * 32, 32), 32)],
                    dst_ref=got.at[n, pl.ds(mine, 32)],
                    send_sem=s_a2a, recv_sem=r_a2a.at[g],
                    device_id=(target, n), device_id_type=MESH,
                ).start()

    @pl.loop(0, 4)
    def _(r):
        plane_copy(w * 4 + r, sib, s_sib).start()

    for copy in small:
        copy.wait()
    lane = lax.broadcasted_iota(jnp.int32, (8, 128), 1)
    sub = lax.broadcasted_iota(jnp.int32, (8, 128), 0)
    where = jnp.full((8, 128), 16, jnp.int32)
    for a in range(4):
        for s in range(16):
            where = jnp.where((sub == a) & (lane == lad_idx[a, s]), s, where)
    inv_v[...] = where
    inv_copy = pltpu.make_async_copy(inv_v, inv, s_inv)
    inv_copy.start()
    acc[...] = jnp.zeros_like(acc)

    def y_copy(direction, item):
        if item < 4:
            where, g = n, item
        elif direction == 0:
            where, g = down, item - 4
        else:
            where, g = up, item - 2
        place = got.at[where, pl.ds(pl.multiple_of(rows[g] * 256, 256), 256)]
        return pltpu.make_async_remote_copy(
            src_ref=place, dst_ref=place, send_sem=s_y.at[direction],
            recv_sem=r_y.at[direction, item],
            device_id=(w, up if direction == 0 else down), device_id_type=MESH,
        )

    def y_in(item):
        for direction in range(2):
            wait_for(got.at[0, pl.ds(0, 256)], r_y.at[direction, item])

    def spread(slice_of, g):
        row = pl.multiple_of(rows[g] * 32, 32)
        for k in range(8):
            high, low = split(got[slice_of, pl.ds(rows[g] * 256 + k, 32, stride=8), :])
            thi[slice_of * 8 + k, pl.ds(row, 32), :] = high
            tlo[slice_of * 8 + k, pl.ds(row, 32), :] = low

    for g in range(4):
        wait_for(got.at[0, pl.ds(0, 224 if g == 0 else 256)], r_a2a.at[g])
        for direction in range(2):
            y_copy(direction, g).start()
        plane_send(g)
        lad_load(g).wait()

        @pl.loop(0, 16)
        def _(s):
            high, low = split(lstage[g % 2, s])
            lhi[g * 17 + s] = high
            llo[g * 17 + s] = low

        lhi[g * 17 + 16] = jnp.zeros((128, 128), BF16)
        llo[g * 17 + 16] = jnp.zeros((128, 128), BF16)
        if g < 2:
            lad_load(g + 2).start()
    for g in range(4):
        spread(n, g)
    inv_copy.wait()

    column = jnp.broadcast_to(ev_row[...], (128, 128)).T
    lanes = lax.broadcasted_iota(jnp.int32, (8, 256), 1)
    first, second = lanes // 32, lax.rem(lanes, 32)
    row_i = jnp.full((8, 256), eo[n * 8], F32)
    for i in range(1, 8):
        row_i = jnp.where(first == i, eo[n * 8 + i], row_i)
    row_j = jnp.full((8, 256), eo[0], F32)
    for j in range(1, 32):
        row_j = jnp.where(second == j, eo[j], row_j)
    base = jnp.concatenate([column, column], axis=1)
    less_i, less_j = row_i[0:1, :], row_j[0:1, :]

    for a in range(4):
        den[a * 128:(a + 1) * 128, :] = (ev[w * 4 + a] + base) - less_i - less_j

    def cycle_terms(slice_of, ip):
        @pl.loop(0, 2)
        def _(ii):
            i = slice_of * 8 + ip * 2 + ii
            blocks = [split(cyc[i, s]) for s in range(4)]
            left_high = jnp.concatenate([b[0] for b in blocks], axis=1)
            left_low = jnp.concatenate([b[1] for b in blocks], axis=1)
            listed = [cyc_idx[s, i] for s in range(4)]
            right_high = jnp.concatenate([thi[k] for k in listed], axis=0)
            right_low = jnp.concatenate([tlo[k] for k in listed], axis=0)
            part[slice_of, ip, ii] = (
                dot(left_high, right_high) + dot(left_low, right_high) + dot(left_high, right_low)
            )

    flip = (0, 2)

    def rs_copy(direction, slot):
        near = up if direction == 0 else down
        target, ip = ((far, 0), (far, 1), (near, 2), (near, 0), (near, 3), (near, 1))[slot]
        return pltpu.make_async_remote_copy(
            src_ref=part.at[target, ip ^ flip[direction]], dst_ref=rbuf.at[direction, slot],
            send_sem=s_rs.at[direction], recv_sem=r_rs.at[direction, slot],
            device_id=(w, near), device_id_type=MESH,
        )

    def rs_send(slot):
        for direction in range(2):
            rs_copy(direction, slot).start()

    def rs_in(slot):
        for direction in range(2):
            wait_for(rbuf.at[direction, slot], r_rs.at[direction, slot])

    def merge(slot):
        rs_in(slot)
        part[up, slot] += rbuf[0, slot]
        part[down, slot ^ 2] += rbuf[1, slot]

    lower = lax.broadcasted_iota(jnp.int32, (8, 128), 0) < 4

    def give_back(half):
        for item in range(2):
            ip = half + 2 * item
            slots = {0: (3, 2), 2: (2, 3), 1: (5, 4), 3: (4, 5)}[ip]
            values = [
                part[n, ip, ii] + rbuf[0, slots[0], ii] + rbuf[1, slots[1], ii] for ii in range(2)
            ]
            for target in range(16):
                first, second = (v[target * 8:target * 8 + 8, :] for v in values)
                row = target * 32 + item * 8
                zsend[half, row:row + 8, :] = jnp.where(lower, first, pltpu.roll(second, 4, 0))
                zsend[half, row + 16:row + 24, :] = jnp.where(
                    lower, pltpu.roll(first, 4, 0), second
                )

        here = pl.multiple_of(w * 16, 16)

        @pl.loop(0, 8)
        def _(m):
            for g in (2, 1, 3, 0):
                @pl.when((lax.rem(m * 3, 8) > 0) | (g > 0))
                def _():
                    target = lax.rem(x + g, SIDE) * 8 + lax.rem(place_in_row + lax.rem(m * 3, 8), 8)
                    pltpu.make_async_remote_copy(
                        src_ref=zsend.at[half, pl.ds(pl.multiple_of(target * 16, 16), 16)],
                        dst_ref=zgot.at[half, pl.ds(here, 16)],
                        send_sem=s_back.at[half], recv_sem=r_back.at[half],
                        device_id=(target, n), device_id_type=MESH,
                    ).start()

        zgot[half, pl.ds(here, 16), :] = zsend[half, pl.ds(here, 16), :]

    def pair(c):
        other = c + 4 - 8 * core
        high_0, low_0 = split(gath[c])
        high_1, low_1 = split(gath[other])
        high = jnp.concatenate([high_0, high_1], axis=0)
        low = jnp.concatenate([low_0, low_1], axis=0)

        def taken(table):
            return jnp.concatenate(
                [
                    jnp.concatenate(
                        [table[a * 17 + inv[a, c]], table[a * 17 + inv[a, other]]], axis=1
                    )
                    for a in range(4)
                ],
                axis=0,
            )

        left_high, left_low = taken(lhi), taken(llo)
        acc[...] += dot(left_high, high) + dot(left_low, high) + dot(left_high, low)

    def pairs_of(q):
        @pl.loop(0, 4)
        def _(d):
            def packed(part_of):
                value = ARRIVE[3][part_of]
                for e in range(3):
                    value = jnp.where(d == e, ARRIVE[e][part_of], value)
                return value

            later = chunk(tuple(packed(part_of) for part_of in range(3)), jnp.maximum(q - 1, 0))
            c = jnp.where(q == 0, w * 4 + d, later)
            other = c + 4 - 8 * core
            wait_for(gath.at[other], r_gath.at[other])
            pair(c)

    @pl.loop(0, SLOTS)
    def _(q):
        for d in range(4):
            c = chunk(ARRIVE[d], q)
            wait_for(gath.at[c], r_gath.at[c])
            plane_copy(c, sib, s_sib).start()

        @pl.when(q == 0)
        def _():
            plane_send(AHEAD - 1)

        @pl.when(q < SLOTS - AHEAD)
        def _():
            plane_send(q + AHEAD)

        @pl.when(q == 0)
        def _():
            for item in range(2):
                y_in(item)
                y_copy(0, 4 + item).start()
                spread(down, item)
                spread(up, item)

        @pl.when(q == 1)
        def _():
            y_in(2)
            y_copy(1, 4).start()
            spread(down, 2)
            spread(up, 2)

        @pl.when(q == 2)
        def _():
            y_in(3)
            y_copy(1, 5).start()
            spread(down, 3)
            spread(up, 3)

        @pl.when(q == 3)
        def _():
            y_in(4)
            spread(far, 0)
            spread(far, 2)

        @pl.when(q == 5)
        def _():
            cyc_load.wait()
            y_in(5)
            spread(far, 1)
            spread(far, 3)
            cycle_terms(far, 0)
            rs_copy(0, 0).start()
            cycle_terms(far, 2)
            rs_copy(1, 0).start()

        @pl.when(q == 6)
        def _():
            cycle_terms(far, 1)
            cycle_terms(far, 3)
            rs_send(1)
            cycle_terms(up, 2)
            cycle_terms(down, 0)
            rs_send(2)

        @pl.when(q == 7)
        def _():
            cycle_terms(up, 0)
            cycle_terms(down, 2)
            merge(0)
            rs_send(3)

        @pl.when(q == 8)
        def _():
            cycle_terms(up, 3)
            cycle_terms(down, 1)
            rs_send(4)

        @pl.when(q == 9)
        def _():
            cycle_terms(up, 1)
            cycle_terms(down, 3)
            merge(1)
            rs_send(5)

        @pl.when(q == 10)
        def _():
            for ip in range(4):
                cycle_terms(n, ip)

        @pl.when(q == 11)
        def _():
            rs_in(2)
            rs_in(3)
            give_back(0)

        @pl.when(q == 13)
        def _():
            rs_in(4)
            rs_in(5)
            give_back(1)

        pairs_of(q)

    pairs_of(SLOTS)

    for d in range(4):
        wait_for(gath.at[pl.ds(0, SLOTS)], s_gath.at[d])
    wait_for(gath.at[pl.ds(0, 64)], s_sib)
    wait_for(snd.at[pl.ds(0, 992)], s_a2a)
    for direction in range(2):
        wait_for(rbuf.at[direction], s_rs.at[direction])
        wait_for(rbuf.at[direction], s_y.at[direction])
    for half in range(2):
        wait_for(zgot.at[half, pl.ds(0, 496)], r_back.at[half])

    for a in range(4):
        term = jnp.concatenate(
            [
                zgot[i // 2 % 2, pl.ds(i // 4 * 8 + i % 2 * 4 + a, 32, stride=16), :]
                for i in range(8)
            ],
            axis=0,
        ).T
        here = slice(a * 128, (a + 1) * 128)
        out_v[here, :] = (acc[here, :] + term) / den[here, :]
        pltpu.make_async_copy(out_v.at[here], out_ref.at[here], s_out.at[a]).start()

    for half in range(2):
        wait_for(zsend.at[half, pl.ds(0, 496)], s_back.at[half])
    for a in range(4):
        here = slice(a * 128, (a + 1) * 128)
        pltpu.make_async_copy(out_v.at[here], out_ref.at[here], s_out.at[a]).wait()


def per_device(
    amplitudes, ladder_blocks, ladder_index, cycle_blocks, cycle_index, eps_virt, eps_occ
):
    hbm = pl.BlockSpec(memory_space=pl.ANY)
    dma = pltpu.SemaphoreType.DMA
    return pl.pallas_call(
        kernel,
        name="doubles",
        out_shape=jax.ShapeDtypeStruct((512, 256), F32),
        in_specs=[hbm] * 8,
        out_specs=hbm,
        scratch_shapes=[
            pltpu.VMEM((128, 128, 256), F32),
            pltpu.VMEM((68, 128, 128), BF16),
            pltpu.VMEM((68, 128, 128), BF16),
            pltpu.VMEM((2, 16, 128, 128), F32),
            pltpu.VMEM((32, 4, 128, 128), F32),
            pltpu.VMEM((1024, 128), F32),
            pltpu.VMEM((1024, 128), F32),
            pltpu.VMEM((4, 1024, 128), F32),
            pltpu.VMEM((32, 128, 128), BF16),
            pltpu.VMEM((32, 128, 128), BF16),
            pltpu.VMEM((4, 4, 2, 128, 128), F32),
            pltpu.VMEM((2, 6, 2, 128, 128), F32),
            pltpu.VMEM((2, 512, 128), F32),
            pltpu.VMEM((2, 512, 128), F32),
            pltpu.VMEM((512, 256), F32),
            pltpu.VMEM((8, 128), jnp.int32),
            pltpu.SMEM((8, 128), jnp.int32),
            pltpu.SMEM((4, 16), jnp.int32),
            pltpu.SMEM((4, 32), jnp.int32),
            pltpu.SMEM((128,), F32),
            pltpu.SMEM((32,), F32),
            pltpu.VMEM((1, 128), F32),
            pltpu.VMEM((512, 256), F32),
            pltpu.VMEM((512, 256), F32),
            dma((5,)), dma, dma, dma((128,)), dma((4,)), dma, dma((2,)), dma,
            dma, dma((4,)), dma((2,)), dma((2, 6)), dma((2,)), dma((2, 6)),
            dma((2,)), dma((2,)), dma((4,)),
        ],
        compiler_params=pltpu.CompilerParams(
            collective_id=0, has_side_effects=True, vmem_limit_bytes=60 << 20
        ),
    )(
        ladder_index, cycle_index.T, eps_virt, eps_occ, amplitudes.reshape(4, 128, 256),
        ladder_blocks, cycle_blocks, eps_virt[None, :],
    )


def solution(mesh):
    in_specs = (
        P("wide", "narrow"),
        P("wide", None, None, None),
        P("wide", None),
        P(None, "narrow", None, None),
        P(None, "narrow"),
        P(),
        P(),
    )
    return jax.shard_map(
        per_device, mesh=mesh, in_specs=in_specs, out_specs=P("wide", "narrow"), check_vma=False
    )
```

```python
import functools

import jax
import jax.numpy as jnp
from jax import lax
from jax.experimental import pallas as pl
from jax.experimental.pallas import tpu as pltpu
from jax.sharding import PartitionSpec as P

MESH = pl.DeviceIdType.MESH
F32 = jnp.float32
BF16 = jnp.bfloat16
SIDE = 4
SLOTS = 15
AHEAD = 5

X_PLUS = (
    (0, 0, 0), (0, 0, 1), (0, 0, 2), (0, 0, 3), (-1, 0, 0),
    (0, -1, 2), (0, -1, 3), (0, 1, 2), (0, 1, 3), (0, 2, 2), (0, 2, 3),
    (-1, 0, 2), (-1, -1, 2), (-1, 1, 2), (-1, 2, 2),
)
X_MINUS = tuple((-dx, -dz, r ^ 1) for dx, dz, r in X_PLUS)
Z_PLUS = tuple((dz, dx, r ^ 2) for dx, dz, r in X_PLUS)
Z_MINUS = tuple((dz, dx, r ^ 2) for dx, dz, r in X_MINUS)
STREAMS = (X_PLUS, X_MINUS, Z_PLUS, Z_MINUS)
STEPS = ((1, 0), (-1, 0), (0, 1), (0, -1))


def digits(values):
    return sum((value % SIDE) << (2 * position) for position, value in enumerate(values))


SEND = tuple(
    tuple(digits([item[part] for item in stream]) for part in range(3)) for stream in STREAMS
)
ARRIVE = tuple(
    tuple(
        digits([item[part] - (step[part] if part < 2 else 0) for item in stream])
        for part in range(3)
    )
    for stream, step in zip(STREAMS, STEPS)
)


def digit(packed, position):
    return lax.rem(lax.shift_right_logical(packed, 2 * position), SIDE)


def split(value):
    high = value.astype(BF16)
    return high, (value - high.astype(F32)).astype(BF16)


def dot(left, right):
    return jnp.dot(left, right, preferred_element_type=F32)


ROWS = (0, 3, 1, 2)


def kernel(
    lad_idx_ref, cyc_idx_ref, ev_ref, eo_ref, t_ref, lad_ref, cyc_ref, ev_row_ref, out_ref,
    gath, lhi, llo, lstage, cyc, turn, snd, got, thi, tlo, part, rbuf, zsend, zgot, acc,
    inv_v, inv, lad_idx, cyc_idx, ev, eo, ev_row, den, out_v,
    s_idx, s_inv, s_own, r_gath, s_gath, s_sib, s_lad, s_cyc, s_a2a, r_a2a, s_y, r_y, s_rs, r_rs,
    s_back, r_back, s_out,
):
    w = lax.axis_index("wide")
    n = lax.axis_index("narrow")
    core = lax.rem(w, 2)
    chip = w // 2
    x = chip // SIDE
    z = lax.rem(chip, SIDE)
    place_in_row = lax.rem(w, 8)
    sib = w + 1 - 2 * core
    up = lax.rem(n + 1, SIDE)
    down = lax.rem(n + 3, SIDE)
    far = lax.rem(n + 2, SIDE)
    wide = 32
    rows = [lax.rem(x + offset, SIDE) for offset in ROWS]

    def wide_of(dx, dz):
        return (lax.rem(x + dx, SIDE) * SIDE + lax.rem(z + dz, SIDE)) * 2 + core

    neighbours = [wide_of(step[0] % SIDE, step[1] % SIDE) for step in STEPS]

    def chunk(packed, position):
        return wide_of(digit(packed[0], position), digit(packed[1], position)) * 4 + digit(
            packed[2], position
        )

    def plane_copy(c, target, send_sem):
        return pltpu.make_async_remote_copy(
            src_ref=gath.at[c], dst_ref=gath.at[c], send_sem=send_sem, recv_sem=r_gath.at[c],
            device_id=(target, n), device_id_type=MESH,
        )

    def wait_for(place, sem):
        pltpu.make_async_copy(place, place, sem).wait()

    barrier = pltpu.get_barrier_semaphore()

    @pl.loop(1, wide)
    def _(k):
        pl.semaphore_signal(
            barrier, inc=1, device_id=(lax.rem(w + k, wide), n), device_id_type=MESH
        )

    for other in (up, down):
        pl.semaphore_signal(barrier, inc=1, device_id=(w, other), device_id_type=MESH)

    own = pltpu.make_async_copy(t_ref, gath.at[pl.ds(w * 4, 4)], s_own)
    own.start()
    small = [
        pltpu.make_async_copy(source, target, s_idx.at[k])
        for k, (source, target) in enumerate(
            (
                (lad_idx_ref, lad_idx), (cyc_idx_ref, cyc_idx), (ev_ref, ev), (eo_ref, eo),
                (ev_row_ref, ev_row),
            )
        )
    ]
    for copy in small:
        copy.start()

    def lad_load(a):
        return pltpu.make_async_copy(lad_ref.at[a], lstage.at[a % 2], s_lad.at[a % 2])

    lad_load(0).start()
    lad_load(1).start()
    cyc_load = pltpu.make_async_copy(cyc_ref, cyc, s_cyc)
    cyc_load.start()

    own.wait()
    for c in range(4):
        turn[c * 256:(c + 1) * 256, :] = gath[w * 4 + c].T

    @pl.loop(0, wide)
    def _(j):
        for c in range(4):
            row = pl.multiple_of(j * 32 + c * 8, 8)
            snd[pl.ds(row, 8), :] = turn[pl.ds(c * 256 + j, 8, stride=32), :]

    mine = pl.multiple_of(w * 32, 32)
    got[n, pl.ds(mine, 32), :] = snd[pl.ds(mine, 32), :]

    def plane_send(s):
        for d in range(4):
            plane_copy(chunk(SEND[d], s), neighbours[d], s_gath.at[d]).start()

    pl.semaphore_wait(barrier, wide + 1)

    @pl.loop(0, 8)
    def _(m):
        for g in (0, 1, 2, 3):
            @pl.when((lax.rem(m * 3, 8) > 0) | (g > 0))
            def _():
                row_of = lax.rem(x + (SIDE - ROWS[g]) % SIDE, SIDE)
                target = row_of * 8 + lax.rem(place_in_row + lax.rem(m * 3, 8), 8)
                pltpu.make_async_remote_copy(
                    src_ref=snd.at[pl.ds(pl.multiple_of(target * 32, 32), 32)],
                    dst_ref=got.at[n, pl.ds(mine, 32)],
                    send_sem=s_a2a, recv_sem=r_a2a.at[g],
                    device_id=(target, n), device_id_type=MESH,
                ).start()

    @pl.loop(0, 4)
    def _(r):
        plane_copy(w * 4 + r, sib, s_sib).start()

    for copy in small:
        copy.wait()
    lane = lax.broadcasted_iota(jnp.int32, (8, 128), 1)
    sub = lax.broadcasted_iota(jnp.int32, (8, 128), 0)
    where = jnp.full((8, 128), 16, jnp.int32)
    for a in range(4):
        for s in range(16):
            where = jnp.where((sub == a) & (lane == lad_idx[a, s]), s, where)
    inv_v[...] = where
    inv_copy = pltpu.make_async_copy(inv_v, inv, s_inv)
    inv_copy.start()
    acc[...] = jnp.zeros_like(acc)

    def y_copy(direction, item):
        if item < 4:
            where, g = n, item
        elif direction == 0:
            where, g = down, item - 4
        else:
            where, g = up, item - 2
        place = got.at[where, pl.ds(pl.multiple_of(rows[g] * 256, 256), 256)]
        return pltpu.make_async_remote_copy(
            src_ref=place, dst_ref=place, send_sem=s_y.at[direction],
            recv_sem=r_y.at[direction, item],
            device_id=(w, up if direction == 0 else down), device_id_type=MESH,
        )

    def y_in(item):
        for direction in range(2):
            wait_for(got.at[0, pl.ds(0, 256)], r_y.at[direction, item])

    def spread(slice_of, g):
        row = pl.multiple_of(rows[g] * 32, 32)
        for k in range(8):
            high, low = split(got[slice_of, pl.ds(rows[g] * 256 + k, 32, stride=8), :])
            thi[slice_of * 8 + k, pl.ds(row, 32), :] = high
            tlo[slice_of * 8 + k, pl.ds(row, 32), :] = low

    for g in range(4):
        wait_for(got.at[0, pl.ds(0, 224 if g == 0 else 256)], r_a2a.at[g])
        for direction in range(2):
            y_copy(direction, g).start()
        plane_send(g)
        lad_load(g).wait()

        @pl.loop(0, 16)
        def _(s):
            high, low = split(lstage[g % 2, s])
            lhi[g * 17 + s] = high
            llo[g * 17 + s] = low

        lhi[g * 17 + 16] = jnp.zeros((128, 128), BF16)
        llo[g * 17 + 16] = jnp.zeros((128, 128), BF16)
        if g < 2:
            lad_load(g + 2).start()
    for g in range(4):
        spread(n, g)
    inv_copy.wait()

    column = jnp.broadcast_to(ev_row[...], (128, 128)).T
    lanes = lax.broadcasted_iota(jnp.int32, (8, 256), 1)
    first, second = lanes // 32, lax.rem(lanes, 32)
    row_i = jnp.full((8, 256), eo[n * 8], F32)
    for i in range(1, 8):
        row_i = jnp.where(first == i, eo[n * 8 + i], row_i)
    row_j = jnp.full((8, 256), eo[0], F32)
    for j in range(1, 32):
        row_j = jnp.where(second == j, eo[j], row_j)
    base = jnp.concatenate([column, column], axis=1)
    less_i, less_j = row_i[0:1, :], row_j[0:1, :]

    for a in range(4):
        den[a * 128:(a + 1) * 128, :] = (ev[w * 4 + a] + base) - less_i - less_j

    def cycle_terms(slice_of, ip):
        @pl.loop(0, 2)
        def _(ii):
            i = slice_of * 8 + ip * 2 + ii
            blocks = [split(cyc[i, s]) for s in range(4)]
            left_high = jnp.concatenate([b[0] for b in blocks], axis=1)
            left_low = jnp.concatenate([b[1] for b in blocks], axis=1)
            listed = [cyc_idx[s, i] for s in range(4)]
            right_high = jnp.concatenate([thi[k] for k in listed], axis=0)
            right_low = jnp.concatenate([tlo[k] for k in listed], axis=0)
            part[slice_of, ip, ii] = (
                dot(left_high, right_high) + dot(left_low, right_high) + dot(left_high, right_low)
            )

    flip = (0, 2)

    def rs_copy(direction, slot):
        near = up if direction == 0 else down
        target, ip = ((far, 0), (far, 1), (near, 2), (near, 0), (near, 3), (near, 1))[slot]
        return pltpu.make_async_remote_copy(
            src_ref=part.at[target, ip ^ flip[direction]], dst_ref=rbuf.at[direction, slot],
            send_sem=s_rs.at[direction], recv_sem=r_rs.at[direction, slot],
            device_id=(w, near), device_id_type=MESH,
        )

    def rs_send(slot):
        for direction in range(2):
            rs_copy(direction, slot).start()

    def rs_in(slot):
        for direction in range(2):
            wait_for(rbuf.at[direction, slot], r_rs.at[direction, slot])

    def merge(slot):
        rs_in(slot)
        part[up, slot] += rbuf[0, slot]
        part[down, slot ^ 2] += rbuf[1, slot]

    lower = lax.broadcasted_iota(jnp.int32, (8, 128), 0) < 4

    def give_back(half):
        for item in range(2):
            ip = half + 2 * item
            slots = {0: (3, 2), 2: (2, 3), 1: (5, 4), 3: (4, 5)}[ip]
            values = [
                part[n, ip, ii] + rbuf[0, slots[0], ii] + rbuf[1, slots[1], ii] for ii in range(2)
            ]
            for target in range(16):
                first, second = (v[target * 8:target * 8 + 8, :] for v in values)
                row = target * 32 + item * 8
                zsend[half, row:row + 8, :] = jnp.where(lower, first, pltpu.roll(second, 4, 0))
                zsend[half, row + 16:row + 24, :] = jnp.where(
                    lower, pltpu.roll(first, 4, 0), second
                )

        here = pl.multiple_of(w * 16, 16)

        @pl.loop(0, 8)
        def _(m):
            for g in (2, 1, 3, 0):
                @pl.when((lax.rem(m * 3, 8) > 0) | (g > 0))
                def _():
                    target = lax.rem(x + g, SIDE) * 8 + lax.rem(place_in_row + lax.rem(m * 3, 8), 8)
                    pltpu.make_async_remote_copy(
                        src_ref=zsend.at[half, pl.ds(pl.multiple_of(target * 16, 16), 16)],
                        dst_ref=zgot.at[half, pl.ds(here, 16)],
                        send_sem=s_back.at[half], recv_sem=r_back.at[half],
                        device_id=(target, n), device_id_type=MESH,
                    ).start()

        zgot[half, pl.ds(here, 16), :] = zsend[half, pl.ds(here, 16), :]

    def pair(c):
        other = c + 4 - 8 * core
        high_0, low_0 = split(gath[c])
        high_1, low_1 = split(gath[other])
        high = jnp.concatenate([high_0, high_1], axis=0)
        low = jnp.concatenate([low_0, low_1], axis=0)

        def taken(table):
            return jnp.concatenate(
                [
                    jnp.concatenate(
                        [table[a * 17 + inv[a, c]], table[a * 17 + inv[a, other]]], axis=1
                    )
                    for a in range(4)
                ],
                axis=0,
            )

        left_high, left_low = taken(lhi), taken(llo)
        acc[...] += dot(left_high, high) + dot(left_low, high) + dot(left_high, low)

    def pairs_of(q):
        @pl.loop(0, 4)
        def _(d):
            def packed(part_of):
                value = ARRIVE[3][part_of]
                for e in range(3):
                    value = jnp.where(d == e, ARRIVE[e][part_of], value)
                return value

            later = chunk(tuple(packed(part_of) for part_of in range(3)), jnp.maximum(q - 1, 0))
            c = jnp.where(q == 0, w * 4 + d, later)
            other = c + 4 - 8 * core
            wait_for(gath.at[other], r_gath.at[other])
            pair(c)

    @pl.loop(0, SLOTS)
    def _(q):
        for d in range(4):
            c = chunk(ARRIVE[d], q)
            wait_for(gath.at[c], r_gath.at[c])
            plane_copy(c, sib, s_sib).start()

        @pl.when(q == 0)
        def _():
            plane_send(AHEAD - 1)

        @pl.when(q < SLOTS - AHEAD)
        def _():
            plane_send(q + AHEAD)

        @pl.when(q == 0)
        def _():
            for item in range(2):
                y_in(item)
                y_copy(0, 4 + item).start()
                spread(down, item)
                spread(up, item)

        @pl.when(q == 1)
        def _():
            y_in(2)
            y_copy(1, 4).start()
            spread(down, 2)
            spread(up, 2)

        @pl.when(q == 2)
        def _():
            y_in(3)
            y_copy(1, 5).start()
            spread(down, 3)
            spread(up, 3)

        @pl.when(q == 3)
        def _():
            y_in(4)
            spread(far, 0)
            spread(far, 2)

        @pl.when(q == 5)
        def _():
            cyc_load.wait()
            y_in(5)
            spread(far, 1)
            spread(far, 3)
            cycle_terms(far, 0)
            rs_copy(0, 0).start()
            cycle_terms(far, 2)
            rs_copy(1, 0).start()

        @pl.when(q == 6)
        def _():
            cycle_terms(far, 1)
            cycle_terms(far, 3)
            rs_send(1)
            cycle_terms(up, 2)
            cycle_terms(down, 0)
            rs_send(2)

        @pl.when(q == 7)
        def _():
            cycle_terms(up, 0)
            cycle_terms(down, 2)
            merge(0)
            rs_send(3)

        @pl.when(q == 8)
        def _():
            cycle_terms(up, 3)
            cycle_terms(down, 1)
            rs_send(4)

        @pl.when(q == 9)
        def _():
            cycle_terms(up, 1)
            cycle_terms(down, 3)
            merge(1)
            rs_send(5)

        @pl.when(q == 10)
        def _():
            for ip in range(4):
                cycle_terms(n, ip)

        @pl.when(q == 10)
        def _():
            rs_in(2)
            rs_in(3)
            give_back(0)

        @pl.when(q == 12)
        def _():
            rs_in(4)
            rs_in(5)
            give_back(1)

        pairs_of(q)

    pairs_of(SLOTS)

    for d in range(4):
        wait_for(gath.at[pl.ds(0, SLOTS)], s_gath.at[d])
    wait_for(gath.at[pl.ds(0, 64)], s_sib)
    wait_for(snd.at[pl.ds(0, 992)], s_a2a)
    for direction in range(2):
        wait_for(rbuf.at[direction], s_rs.at[direction])
        wait_for(rbuf.at[direction], s_y.at[direction])
    for half in range(2):
        wait_for(zgot.at[half, pl.ds(0, 496)], r_back.at[half])

    for a in range(4):
        term = jnp.concatenate(
            [
                zgot[i // 2 % 2, pl.ds(i // 4 * 8 + i % 2 * 4 + a, 32, stride=16), :]
                for i in range(8)
            ],
            axis=0,
        ).T
        here = slice(a * 128, (a + 1) * 128)
        out_v[here, :] = (acc[here, :] + term) / den[here, :]
        pltpu.make_async_copy(out_v.at[here], out_ref.at[here], s_out.at[a]).start()

    for half in range(2):
        wait_for(zsend.at[half, pl.ds(0, 496)], s_back.at[half])
    for a in range(4):
        here = slice(a * 128, (a + 1) * 128)
        pltpu.make_async_copy(out_v.at[here], out_ref.at[here], s_out.at[a]).wait()


def per_device(
    amplitudes, ladder_blocks, ladder_index, cycle_blocks, cycle_index, eps_virt, eps_occ
):
    hbm = pl.BlockSpec(memory_space=pl.ANY)
    dma = pltpu.SemaphoreType.DMA
    return pl.pallas_call(
        kernel,
        name="doubles",
        out_shape=jax.ShapeDtypeStruct((512, 256), F32),
        in_specs=[hbm] * 8,
        out_specs=hbm,
        scratch_shapes=[
            pltpu.VMEM((128, 128, 256), F32),
            pltpu.VMEM((68, 128, 128), BF16),
            pltpu.VMEM((68, 128, 128), BF16),
            pltpu.VMEM((2, 16, 128, 128), F32),
            pltpu.VMEM((32, 4, 128, 128), F32),
            pltpu.VMEM((1024, 128), F32),
            pltpu.VMEM((1024, 128), F32),
            pltpu.VMEM((4, 1024, 128), F32),
            pltpu.VMEM((32, 128, 128), BF16),
            pltpu.VMEM((32, 128, 128), BF16),
            pltpu.VMEM((4, 4, 2, 128, 128), F32),
            pltpu.VMEM((2, 6, 2, 128, 128), F32),
            pltpu.VMEM((2, 512, 128), F32),
            pltpu.VMEM((2, 512, 128), F32),
            pltpu.VMEM((512, 256), F32),
            pltpu.VMEM((8, 128), jnp.int32),
            pltpu.SMEM((8, 128), jnp.int32),
            pltpu.SMEM((4, 16), jnp.int32),
            pltpu.SMEM((4, 32), jnp.int32),
            pltpu.SMEM((128,), F32),
            pltpu.SMEM((32,), F32),
            pltpu.VMEM((1, 128), F32),
            pltpu.VMEM((512, 256), F32),
            pltpu.VMEM((512, 256), F32),
            dma((5,)), dma, dma, dma((128,)), dma((4,)), dma, dma((2,)), dma,
            dma, dma((4,)), dma((2,)), dma((2, 6)), dma((2,)), dma((2, 6)),
            dma((2,)), dma((2,)), dma((4,)),
        ],
        compiler_params=pltpu.CompilerParams(
            collective_id=0, has_side_effects=True, vmem_limit_bytes=60 << 20
        ),
    )(
        ladder_index, cycle_index.T, eps_virt, eps_occ, amplitudes.reshape(4, 128, 256),
        ladder_blocks, cycle_blocks, eps_virt[None, :],
    )


def solution(mesh):
    in_specs = (
        P("wide", "narrow"),
        P("wide", None, None, None),
        P("wide", None),
        P(None, "narrow", None, None),
        P(None, "narrow"),
        P(),
        P(),
    )
    return jax.shard_map(
        per_device, mesh=mesh, in_specs=in_specs, out_specs=P("wide", "narrow"), check_vma=False
    )
```
